32 devices in a mesh: dp: 2 (over x), seq: 16 (over z, y, core).
Axes of the slice: x: 2, y: 2, z: 4, core: 2. Of those that a mesh axis runs over, the one named last changes fastest.
Arguments:
- hidden: bfloat16 [2, 2048, 2048], P('dp', 'seq'), may hold values from -7 to 7
- cotangent: bfloat16 [2, 2048, 2048], P('dp', 'seq'), may hold values from -6 to 6
- picks: int32 [2, 2048], P('dp', 'seq'), may hold values from 0 to 1, as said below
- gain: float32 [2048], replicated, may hold values from 0.5 to 1.5
- router: float32 [2048], replicated, may hold values from -0.125 to 0.125
- w_query: bfloat16 [2048, 1024], P('seq'), may hold values from -2 to 2
- w_kv: bfloat16 [2048, 256], P('seq'), may hold values from -2 to 2
- w_out: bfloat16 [1024, 2048], P('seq'), may hold values from -0.1875 to 0.1875
Outputs:
- mixed: bfloat16 [2, 2048, 2048], P('dp', 'seq')
- input_grad: bfloat16 [2, 2048, 2048], P('dp', 'seq')
- kv_grad: float32 [2048, 256], P('seq')
- router_grad: float32 [2048], P('seq')
The draws below stay inside these ranges and needn't reach their ends.
Inputs may be any that keep to these rules, and one draw needn't show every extreme that they name: `picks`: every sequence has exactly 256 picked tokens; each aligned block of 128 tokens has 0 to 32 of them, and in every sequence some block has exactly 32.
All inputs are finite; a program needn't handle non-finite values.
Results may differ from the reference program's by a relative error of at most 0.013.
The reference program's roundings to bfloat16 on the way count: a program that leaves them out, or rounds other values in their place, can miss the bound.
Values may be sent and summed in bfloat16 or wider, within the bound.
No kernel may reach another device: no remote copies, remote signals or barrier semaphores. Data moves between devices by JAX's collectives and lax.ppermute only.
A program may use at most 64 MiB of HBM per device.

```python
import jax
import jax.numpy as jnp
from jax import lax

MODEL_WIDTH = 2048
QUERY_HEADS = 16
KEY_VALUE_HEADS = 2
HEAD_SIZE = 64
TOK_DEV = 128
CAP = 16
LEN = 2048
NSEQ = 2
N_SEQ = 16


def draw_picks(key, part):
    half_count = N_SEQ // 2
    most_picks = 2 * CAP
    key_low, key_pair, key_flip, key_order = jax.random.split(key, 4)
    lower = jax.random.randint(key_low, (NSEQ, half_count), 0, most_picks + 1)
    chosen_pair = jax.random.randint(key_pair, (NSEQ, 1), 0, half_count)
    pair_index = lax.broadcasted_iota(jnp.int32, (NSEQ, half_count), 1)
    lower = jnp.where(pair_index == chosen_pair, most_picks, lower)
    flipped = jax.random.randint(key_flip, (NSEQ, half_count), 0, 2)
    leading = jnp.where(flipped == 1, most_picks - lower, lower)
    counts = jnp.stack([leading, most_picks - leading], axis=2).reshape(NSEQ, N_SEQ)
    order_keys = jax.random.split(key_order, NSEQ * N_SEQ)
    orders = jax.vmap(lambda single: jax.random.permutation(single, TOK_DEV))(order_keys)
    orders = orders.reshape(NSEQ, N_SEQ, TOK_DEV)
    chosen = (orders < counts[:, :, None]).astype(jnp.int32)
    return chosen.reshape(NSEQ, LEN)


def draw_hidden(key, part):
    values = jax.random.truncated_normal(jax.random.fold_in(key, 31), -6.0, 6.0, (NSEQ, LEN, MODEL_WIDTH), jnp.float32)
    return values.astype(jnp.bfloat16)


def draw_w_query(key, part):
    weight_params = jax.random.truncated_normal(jax.random.fold_in(key, 41), -6.0, 6.0, (MODEL_WIDTH, QUERY_HEADS * HEAD_SIZE), jnp.float32) * MODEL_WIDTH ** (-0.5)
    return weight_params.astype(jnp.bfloat16)


def draw_w_kv(key, part):
    weight_params = jax.random.truncated_normal(jax.random.fold_in(key, 43), -6.0, 6.0, (MODEL_WIDTH, 2 * KEY_VALUE_HEADS * HEAD_SIZE), jnp.float32) * MODEL_WIDTH ** (-0.5)
    return weight_params.astype(jnp.bfloat16)


def shard_levels(key, dims, cuts, low, top_value):
    def one(position, parts):
        heights = jax.random.uniform(jax.random.fold_in(jax.random.fold_in(key, 6), position), (parts,), jnp.float32, low / len(cuts), top_value / len(cuts))
        return jnp.repeat(jnp.exp(heights), dims[position] // parts).reshape((-1,) + (1,) * (len(dims) - position - 1))

    factor_of = one(*cuts[0])
    for cut in cuts[1:]:
        factor_of = factor_of * one(*cut)
    return factor_of


def gaussian(stream_key, shape, width, bound, pieces=(), held_as=jnp.bfloat16):
    level = shard_levels(stream_key, shape, pieces, -0.22, 0.18) if pieces else 1.0
    array = jax.random.normal(stream_key, shape, jnp.float32) * width * level
    return jnp.minimum(jnp.maximum(array, -bound), bound).astype(held_as)


def setup_inputs(seed: int = 0) -> dict:
    seeds = jax.random.split(jax.random.key(seed), 9)
    return {
        "hidden": draw_hidden(jax.random.fold_in(seeds[8], 71), 0),
        "cotangent": gaussian(seeds[1], (NSEQ, LEN, MODEL_WIDTH), 1.0, 6.0, ((0, 2), (1, 16))),
        "picks": draw_picks(jax.random.fold_in(seeds[8], 71), 0),
        "gain": jnp.clip(1.0 + 0.1 * jax.random.normal(seeds[3], (MODEL_WIDTH,), jnp.float32), 0.5, 1.5),
        "router": gaussian(seeds[4], (MODEL_WIDTH,), MODEL_WIDTH ** -0.5, 0.125, (), jnp.float32),
        "w_query": draw_w_query(jax.random.fold_in(seeds[8], 71), 0),
        "w_kv": draw_w_kv(jax.random.fold_in(seeds[8], 71), 0),
        "w_out": gaussian(seeds[7], (QUERY_HEADS * HEAD_SIZE, MODEL_WIDTH), (QUERY_HEADS * HEAD_SIZE) ** -0.5, 0.1875, ((0, 16),)),
    }


EPSILON = 1e-05

def dot_transposed(left, right):
    return lax.dot_general(left, right, (((1,), (1,)), ((), ())), preferred_element_type=jnp.float32)

def sequence_pass(hidden_seq, cotangent_seq, pick_seq, gain, router, w_query, w_kv, w_out):
    key_value_width = KEY_VALUE_HEADS * HEAD_SIZE
    query_group_size = QUERY_HEADS // KEY_VALUE_HEADS
    head_scale = HEAD_SIZE ** (-0.5)
    picked_token_count = CAP * N_SEQ
    token_rows = hidden_seq.astype(jnp.float32)
    grad_rows = cotangent_seq.astype(jnp.float32)
    picked_index = jnp.nonzero(pick_seq, size=picked_token_count)[0].astype(jnp.int32)
    gate_prob = jax.nn.sigmoid(jnp.dot(token_rows, router, precision=lax.Precision.HIGHEST))
    block_float = hidden_seq[picked_index].astype(jnp.float32)
    inv_norm = lax.rsqrt(lax.optimization_barrier(jnp.mean(block_float * block_float, axis=1, keepdims=True)) + EPSILON)
    normed = (block_float * inv_norm * gain[None, :]).astype(jnp.bfloat16)
    query_head_rows = jnp.dot(normed, w_query, preferred_element_type=jnp.float32).astype(jnp.bfloat16)
    key_value_pair = jnp.dot(normed, w_kv, preferred_element_type=jnp.float32).astype(jnp.bfloat16)
    key_head_rows = key_value_pair[:, :key_value_width].reshape(picked_token_count, KEY_VALUE_HEADS, HEAD_SIZE).astype(jnp.float32)
    value_head_rows = key_value_pair[:, key_value_width:].reshape(picked_token_count, KEY_VALUE_HEADS, HEAD_SIZE).astype(jnp.float32)
    query_split_parts = query_head_rows.reshape(picked_token_count, KEY_VALUE_HEADS, query_group_size, HEAD_SIZE).astype(jnp.float32)
    ranks = jnp.arange(picked_token_count)
    allowed = (ranks[None, :] <= ranks[:, None])[:, None, None, :]
    scores = jnp.einsum('cgrd,ngd->cgrn', query_split_parts, key_head_rows) * head_scale
    scores = jnp.where(allowed, scores, -jnp.inf)
    score_top = lax.optimization_barrier(jnp.max(scores, axis=3, keepdims=True))
    score_exp = jnp.exp(scores - score_top)
    attn_probs = score_exp / lax.optimization_barrier(jnp.sum(score_exp, axis=3, keepdims=True))
    probs_half = attn_probs.astype(jnp.bfloat16)
    mixed_heads = jnp.einsum('cgrn,ngd->cgrd', probs_half.astype(jnp.float32), value_head_rows)
    mixed_heads = mixed_heads.astype(jnp.bfloat16).reshape(picked_token_count, QUERY_HEADS * HEAD_SIZE)
    block_out = jnp.dot(mixed_heads, w_out, preferred_element_type=jnp.float32).astype(jnp.bfloat16)
    out_tokens = jnp.zeros(token_rows.shape, jnp.float32).at[picked_index].set(block_out.astype(jnp.float32))
    mixed = (token_rows + gate_prob[:, None] * out_tokens).astype(jnp.bfloat16)
    scaled_grad = (gate_prob[:, None] * grad_rows).astype(jnp.bfloat16)
    through = lax.optimization_barrier(jnp.sum(grad_rows * out_tokens, axis=1))
    grad_logit = through * gate_prob * (1.0 - gate_prob)
    router_part = jnp.dot(grad_logit, token_rows, precision=lax.Precision.HIGHEST)
    gradient_heads = dot_transposed(scaled_grad[picked_index], w_out).astype(jnp.bfloat16)
    gradient_split = gradient_heads.reshape(picked_token_count, KEY_VALUE_HEADS, query_group_size, HEAD_SIZE).astype(jnp.float32)
    grad_probs = jnp.einsum('cgrd,ngd->cgrn', gradient_split, value_head_rows)
    inner_sum = lax.optimization_barrier(jnp.sum(attn_probs * grad_probs, axis=3, keepdims=True))
    grad_scores = (attn_probs * (grad_probs - inner_sum)).astype(jnp.bfloat16).astype(jnp.float32)
    grad_query = (jnp.einsum('cgrn,ngd->cgrd', grad_scores, key_head_rows) * head_scale).astype(jnp.bfloat16)
    grad_query = grad_query.reshape(picked_token_count, QUERY_HEADS * HEAD_SIZE)
    grad_keys = jnp.einsum('cgrn,cgrd->ngd', grad_scores, query_split_parts) * head_scale
    grad_values = jnp.einsum('cgrn,cgrd->ngd', probs_half.astype(jnp.float32), gradient_split)
    grad_kv = jnp.concatenate([grad_keys.reshape(picked_token_count, key_value_width), grad_values.reshape(picked_token_count, key_value_width)], axis=1).astype(jnp.bfloat16)
    grad_normed = dot_transposed(grad_query, w_query) + dot_transposed(grad_kv, w_kv)
    upstream = grad_normed * gain[None, :]
    grad_block = inv_norm * upstream - block_float * inv_norm ** 3 * lax.optimization_barrier(jnp.mean(upstream * block_float, axis=1, keepdims=True))
    grad_block = grad_block.astype(jnp.bfloat16)
    kv_part = lax.dot_general(normed, grad_kv, (((0,), (0,)), ((), ())), preferred_element_type=jnp.float32)
    grad_tokens = jnp.zeros(token_rows.shape, jnp.float32).at[picked_index].set(grad_block.astype(jnp.float32))
    input_grad = (grad_rows + grad_logit[:, None] * router[None, :] + grad_tokens).astype(jnp.bfloat16)
    return (mixed, input_grad, kv_part, router_part)

def reference(hidden, cotangent, picks, gain, router, w_query, w_kv, w_out):

    def per_sequence(members):
        return sequence_pass(members[0], members[1], members[2], gain, router, w_query, w_kv, w_out)
    mixed, input_grad, kv_parts, router_parts = lax.map(per_sequence, (hidden, cotangent, picks))
    return (mixed, input_grad, lax.optimization_barrier(jnp.sum(kv_parts, axis=0)), lax.optimization_barrier(jnp.sum(router_parts, axis=0)))
```

```python
import functools

import jax
import jax.numpy as jnp
from jax import lax
from jax.experimental import pallas as pl
from jax.experimental.pallas import tpu as pltpu
from jax.sharding import Mesh, PartitionSpec as P

MODEL_WIDTH = 2048
QUERY_HEADS = 16
KEY_VALUE_HEADS = 2
HEAD_SIZE = 64
GROUP = QUERY_HEADS // KEY_VALUE_HEADS
KV_WIDTH = 2 * KEY_VALUE_HEADS * HEAD_SIZE
Q_WIDTH = QUERY_HEADS * HEAD_SIZE
EPSILON = 1e-05
EMPTY = 2.0**100
PLANE = 4
SEQ = ("zz", "pp")

F32 = jnp.float32
BF16 = jnp.bfloat16


def dot(a, b, ca=1, cb=0):
    return lax.dot_general(a, b, (((ca,), (cb,)), ((), ())), preferred_element_type=F32)


def iota(shape, dim):
    return lax.broadcasted_iota(jnp.int32, shape, dim)


def call(body, name, out_shape, *args, scalars=(), scratch=()):
    vmem = pl.BlockSpec(memory_space=pltpu.VMEM)
    smem = pl.BlockSpec(memory_space=pltpu.SMEM)
    return pl.pallas_call(
        body,
        name=name,
        out_shape=out_shape,
        in_specs=[smem] * len(scalars) + [vmem] * len(args),
        out_specs=jax.tree.map(lambda _: vmem, out_shape),
        scratch_shapes=list(scratch),
    )(*scalars, *args)


def shaped(shape, dtype):
    return jax.ShapeDtypeStruct(shape, dtype)


def selection(picks, slots):
    tokens = picks.shape[1]
    picked = jnp.broadcast_to(picks.astype(F32), (8, tokens)).astype(BF16)
    before = (iota((tokens, tokens), 0) < iota((tokens, tokens), 1)).astype(F32).astype(BF16)
    rank = dot(picked, before)[:1].astype(jnp.int32)
    hit = (iota((slots, tokens), 0) == rank) & (picks > 0)
    return hit.astype(F32).astype(BF16)


def pick_kernel(h_ref, c_ref, picks_ref, gain_ref, router_ref, send_ref, gate_ref, x_ref, inv_ref, *, slots, fb):
    lines = send_ref.shape[0] // PLANE
    hidden = h_ref[...].astype(F32)
    logit = jnp.sum(hidden * router_ref[...], axis=1, keepdims=True)
    gate = 1.0 / (1.0 + jnp.exp(-logit))
    gate_ref[...] = gate
    picks = picks_ref[...]
    sel = selection(picks, slots)
    scaled = (gate * c_ref[...].astype(F32)).astype(BF16)
    x = dot(sel, h_ref[...])
    grads = dot(sel, scaled).astype(BF16)
    inv = lax.rsqrt(jnp.mean(x * x, axis=1, keepdims=True) + EPSILON)
    x_ref[...] = x.astype(BF16)
    inv_ref[...] = inv
    normed = x * inv * gain_ref[...]
    count = jnp.sum(picks)
    normed = jnp.where(iota((slots, 1), 0) < count, normed, EMPTY).astype(BF16)
    for p in range(PLANE):
        blocks = [slice((PLANE * z + p) * fb, (PLANE * z + p + 1) * fb) for z in range(lines)]
        part = jnp.concatenate([normed[:, b] for b in blocks] + [grads[:, b] for b in blocks], axis=1)
        for z in range(lines):
            send_ref[PLANE * z + p] = part


def heads_kernel(
    p_ref, got_ref, wqkv_ref, wout_ref, keep_ref, send_ref, keep_kv_ref, send_kv_ref, normed_ref, place_ref, *, rows, cpd, kpd
):
    slots, width = got_ref.shape
    half = width // 2
    valid = got_ref[:, :1].astype(F32) < EMPTY / 2
    ones = jnp.broadcast_to(jnp.where(valid, 1.0, 0.0), (slots, 128)).astype(BF16)
    earlier = (iota((slots, slots), 1) < iota((slots, slots), 0)).astype(F32).astype(BF16)
    rank = dot(earlier, ones)[:, :1].astype(jnp.int32)
    rank = jnp.where(valid, rank, -1)
    place = (rank == iota((slots, rows), 1)).astype(F32).astype(BF16)
    place_ref[...] = place
    compact = dot(place, got_ref[...], 0, 0).astype(BF16)
    normed, grads = compact[:, :half], compact[:, half:]
    lines, _, fb = normed_ref.shape
    for z in range(lines):
        normed_ref[z] = normed[:, z * fb : (z + 1) * fb]
    query = dot(normed, wqkv_ref[:, : PLANE * cpd])
    grad_heads = dot(grads, wout_ref[...], 1, 1)
    kv = dot(wqkv_ref[:, PLANE * cpd :], normed, 0, 1)
    for pp in range(PLANE):
        cols = slice(pp * cpd, (pp + 1) * cpd)
        both = jnp.concatenate([query[:, cols], grad_heads[:, cols]], axis=1)
        kv_part = kv[pp * kpd : (pp + 1) * kpd]
        away = p_ref[0] ^ pp

        @pl.when(away % 2 == 0)
        def _():
            keep_ref[away // 2] = both
            keep_kv_ref[away // 2] = kv_part

        @pl.when(away % 2 == 1)
        def _():
            send_ref[away // 2] = both
            send_kv_ref[away // 2] = kv_part


def attention_kernel(
    z_ref, qg_ref, kv_ref, wq_ref, wkv_ref, wout_ref, gain_ref, normed_ref, place_ref,
    send_ref, kvg_ref, mixed_ref, gq_ref, gkv_ref, *, step
):
    rows = qg_ref.shape[1]
    n, slots, _ = send_ref.shape
    fb = wq_ref.shape[0]
    scale = HEAD_SIZE**-0.5
    span = GROUP // 2
    gkv_ref[...] = jnp.zeros(gkv_ref.shape, F32)

    def one_head(head, group, start):
        kt = kv_ref[pl.ds(group * HEAD_SIZE, HEAD_SIZE), :]
        vt = kv_ref[pl.ds((KEY_VALUE_HEADS + group) * HEAD_SIZE, HEAD_SIZE), :]
        zero = jnp.zeros_like(kt)
        qg = qg_ref[head, pl.ds(start, step), :]
        scores = dot(qg, jnp.concatenate([kt, zero], axis=0)) * scale
        allowed = iota((step, rows), 1) <= iota((step, rows), 0) + start
        scores = jnp.where(allowed, scores, -jnp.inf)
        e = jnp.exp(scores - jnp.max(scores, axis=1, keepdims=True))
        probs = e / jnp.sum(e, axis=1, keepdims=True)
        probs_half = probs.astype(BF16)
        mixed = dot(probs_half, vt, 1, 1)
        gp = dot(qg, jnp.concatenate([zero, vt], axis=0))
        inner = jnp.sum(probs * gp, axis=1, keepdims=True)
        gs = (probs * (gp - inner)).astype(BF16)
        gq = dot(gs, kt, 1, 1) * scale
        gk = dot(qg, gs, 0, 0)[:HEAD_SIZE] * scale
        gv = dot(qg, probs_half, 0, 0)[HEAD_SIZE:]
        gkv_ref[pl.ds(group * HEAD_SIZE, HEAD_SIZE), :] += gk
        gkv_ref[pl.ds((KEY_VALUE_HEADS + group) * HEAD_SIZE, HEAD_SIZE), :] += gv
        return mixed, gq

    def pair(j, start):
        group = j // span
        m0, g0 = one_head(2 * j, group, start)
        m1, g1 = one_head(2 * j + 1, group, start)
        lanes = pl.ds(j * 2 * HEAD_SIZE, 2 * HEAD_SIZE)
        mixed_ref[pl.ds(start, step), lanes] = jnp.concatenate([m0, m1], axis=1).astype(BF16)
        gq_ref[pl.ds(start, step), lanes] = jnp.concatenate([g0, g1], axis=1).astype(BF16)

    if rows == step:
        for j in range(QUERY_HEADS // 2):
            pair(j, 0)
    else:

        @pl.loop(0, QUERY_HEADS // 2)
        def _(j):
            @pl.loop(0, rows // step)
            def _(b):
                pair(j, pl.multiple_of(b * step, step))

    place = place_ref[...]
    out = dot(mixed_ref[...], wout_ref[...]).astype(BF16)
    gkv = gkv_ref[...].astype(BF16)
    up = (dot(gq_ref[...], wq_ref[...], 1, 1) + dot(gkv, wkv_ref[...], 0, 1)) * gain_ref[...]
    kvg_ref[...] = dot(normed_ref[z_ref[0]], gkv, 0, 1)
    high = up.astype(BF16)
    low = (up - high.astype(F32)).astype(BF16)
    for k, piece in enumerate((out, high, low)):
        spread = dot(place, piece).astype(BF16)
        for d in range(n):
            send_ref[d, :, k * fb : (k + 1) * fb] = spread[d * slots : (d + 1) * slots]


def finish_kernel(
    h_ref, c_ref, picks_ref, router_ref, gate_ref, x_ref, inv_ref, got_ref, mixed_ref, grad_ref, router_grad_ref
):
    n, slots, width = got_ref.shape
    fb = width // 3
    sel = selection(picks_ref[...], slots)
    take = lambda k: jnp.concatenate([got_ref[d, :, k * fb : (k + 1) * fb] for d in range(n)], axis=1)
    out = dot(sel, take(0), 0, 0)
    gate = gate_ref[...]
    hidden = h_ref[...].astype(F32)
    cotangent = c_ref[...].astype(F32)
    mixed_ref[...] = (hidden + gate * out).astype(BF16)
    through = jnp.sum(cotangent * out, axis=1, keepdims=True)
    grad_logit = through * gate * (1.0 - gate)
    router_grad_ref[...] = jnp.sum(grad_logit * hidden, axis=0, keepdims=True)
    up = take(1).astype(F32) + take(2).astype(F32)
    x = x_ref[...].astype(F32)
    inv = inv_ref[...]
    grad_block = inv * up - x * inv**3 * jnp.mean(up * x, axis=1, keepdims=True)
    grad_tokens = dot(sel, grad_block.astype(BF16), 0, 0)
    grad_ref[...] = (cotangent + grad_logit * router_ref[...] + grad_tokens).astype(BF16)


def swap(x, n, bit):
    return lax.ppermute(x, SEQ, [(i, i ^ bit) for i in range(n)])


def local(hidden, cotangent, picks, gain, router, w_query, w_kv, w_out):
    lines = lax.axis_size("zz")
    n = lines * PLANE
    dp = lax.axis_size("dp")
    z, p = lax.axis_index("zz"), lax.axis_index("pp")
    me = (PLANE * z + p).astype(jnp.int32)
    hidden, cotangent = hidden[0], cotangent[0]
    tokens = hidden.shape[0]
    slots = tokens // 4
    rows = n * (tokens // 8)
    fb = MODEL_WIDTH // n
    cpd = Q_WIDTH // n
    kpd = KV_WIDTH // n
    as_row = lambda v: v.reshape(1, -1)
    scalar = lambda v: v.astype(jnp.int32).reshape(1)

    wqkv = jnp.concatenate(
        [w_query.reshape(fb, lines, PLANE * cpd), w_kv.reshape(fb, lines, PLANE * kpd)], axis=2
    ).transpose(1, 0, 2)
    wqkv = lax.all_to_all(wqkv, "zz", 0, 0, tiled=True).reshape(lines * fb, PLANE * (cpd + kpd))
    wout_rows = w_out.reshape(cpd, lines, PLANE, fb).transpose(2, 0, 1, 3).reshape(PLANE, cpd, lines * fb)
    wout_rows = lax.all_to_all(wout_rows, "pp", 0, 0, tiled=True).reshape(PLANE * cpd, lines * fb)
    wout_cols = w_out.reshape(cpd, n, fb).transpose(1, 0, 2)
    wout_cols = lax.all_to_all(wout_cols, SEQ, 0, 0, tiled=True).reshape(Q_WIDTH, fb)

    send, gate, x, inv = call(
        functools.partial(pick_kernel, slots=slots, fb=fb),
        "pick",
        (
            shaped((n, slots, 2 * lines * fb), BF16),
            shaped((tokens, 1), F32),
            shaped((slots, MODEL_WIDTH), BF16),
            shaped((slots, 1), F32),
        ),
        hidden,
        cotangent,
        picks,
        as_row(gain),
        as_row(router),
    )
    got = lax.all_to_all(send, SEQ, 0, 0, tiled=True).reshape(n * slots, 2 * lines * fb)
    qg_shape, kv_shape = (2, rows, 2 * cpd), (2, kpd, rows)
    keep, away, keep_kv, away_kv, normed, place = call(
        functools.partial(heads_kernel, rows=rows, cpd=cpd, kpd=kpd),
        "heads",
        (
            shaped(qg_shape, F32),
            shaped(qg_shape, F32),
            shaped(kv_shape, F32),
            shaped(kv_shape, F32),
            shaped((lines, rows, fb), BF16),
            shaped((n * slots, rows), BF16),
        ),
        got,
        wqkv,
        wout_rows,
        scalars=(scalar(p),),
    )
    keep = keep + swap(away, n, 1)
    keep_kv = keep_kv + swap(away_kv, n, 1)
    qg = (keep[0] + swap(keep[1], n, 2)).astype(BF16)
    kv = (keep_kv[0] + swap(keep_kv[1], n, 2)).astype(BF16)
    packed = jnp.concatenate([qg, kv.reshape(-1, 2 * cpd)], axis=0)

    everything = packed[None]
    if lines == 4:
        everything = jnp.stack([packed] + [swap(packed, n, PLANE * k) for k in range(1, lines)])
        everything = jnp.concatenate([everything[k : k + 1] for k in range(lines)], axis=0)
        index = z ^ jnp.arange(lines)
        everything = everything[index]
    else:
        everything = lax.all_gather(packed, "zz", axis=0)
    everything = everything[:, None]
    for bit in (2, 1):
        other = swap(everything, n, bit)
        first = (p & bit) == 0
        everything = jnp.where(
            first,
            jnp.concatenate([everything, other], axis=1),
            jnp.concatenate([other, everything], axis=1),
        )
    everything = everything.reshape((lines, 2, 2) + packed.shape).transpose(0, 2, 1, 3, 4)
    everything = everything.reshape((n,) + packed.shape)
    qg_all = everything[:, :rows]
    kv_all = everything[:, rows:].reshape(KV_WIDTH, rows)
    if cpd != HEAD_SIZE:
        per = HEAD_SIZE // cpd
        qg_all = qg_all.reshape(QUERY_HEADS, per, rows, 2, cpd).transpose(0, 2, 3, 1, 4)
        qg_all = qg_all.reshape(QUERY_HEADS, rows, 2 * HEAD_SIZE)

    send, kv_part = call(
        functools.partial(attention_kernel, step=min(rows, 256)),
        "attention",
        (shaped((n, slots, 3 * fb), BF16), shaped((fb, KV_WIDTH), F32)),
        qg_all,
        kv_all,
        w_query,
        w_kv,
        wout_cols,
        as_row(lax.dynamic_slice(gain, (me * fb,), (fb,))),
        normed,
        place,
        scalars=(scalar(z),),
        scratch=(
            pltpu.VMEM((rows, Q_WIDTH), BF16),
            pltpu.VMEM((rows, Q_WIDTH), BF16),
            pltpu.VMEM((KV_WIDTH, rows), F32),
        ),
    )
    got = lax.all_to_all(send, SEQ, 0, 0, tiled=True)
    if dp == 2:
        kv_grad = kv_part + lax.ppermute(kv_part, "dp", [(0, 1), (1, 0)])
    else:
        kv_grad = lax.psum(kv_part, "dp")
    mixed, input_grad, router_part = call(
        finish_kernel,
        "finish",
        (
            shaped((tokens, MODEL_WIDTH), BF16),
            shaped((tokens, MODEL_WIDTH), BF16),
            shaped((1, MODEL_WIDTH), F32),
        ),
        hidden,
        cotangent,
        picks,
        as_row(router),
        gate,
        x,
        inv,
        got,
    )
    parts = jnp.broadcast_to(router_part.reshape(1, n, fb), (dp, n, fb)).reshape(dp * n, fb)
    parts = lax.all_to_all(parts, ("dp",) + SEQ, 0, 0, tiled=True)
    router_grad = jnp.sum(parts, axis=0)
    return mixed[None], input_grad[None], kv_grad, router_grad


def solution(mesh):
    dp, n = mesh.shape["dp"], mesh.shape["seq"]
    split = Mesh(mesh.devices.reshape(dp, n // PLANE, PLANE), ("dp",) + SEQ)
    rows = P("dp", SEQ, None)
    return jax.shard_map(
        local,
        mesh=split,
        in_specs=(rows, rows, P("dp", SEQ), P(), P(), P(SEQ, None), P(SEQ, None), P(SEQ, None)),
        out_specs=(rows, rows, P(SEQ, None), P(SEQ)),
        check_vma=False,
    )
```

```python
import functools

import jax
import jax.numpy as jnp
from jax import lax
from jax.experimental import pallas as pl
from jax.experimental.pallas import tpu as pltpu
from jax.sharding import Mesh, PartitionSpec as P


MODEL_WIDTH = 2048
QUERY_HEADS = 16
KEY_VALUE_HEADS = 2
HEAD_SIZE = 64
GROUP = QUERY_HEADS // KEY_VALUE_HEADS
KV_WIDTH = 2 * KEY_VALUE_HEADS * HEAD_SIZE
Q_WIDTH = QUERY_HEADS * HEAD_SIZE
EPSILON = 1e-05
EMPTY = 2.0**100
PLANE = 4
LINES = ("zz", "yy")
SEQ = LINES + ("cc",)

F32 = jnp.float32
BF16 = jnp.bfloat16


def dot(a, b, ca=1, cb=0):
    return lax.dot_general(a, b, (((ca,), (cb,)), ((), ())), preferred_element_type=F32)


def iota(shape, dim):
    return lax.broadcasted_iota(jnp.int32, shape, dim)


def call(body, out_shape, *args, scalars=(), scratch=()):
    vmem = pl.BlockSpec(memory_space=pltpu.VMEM)
    smem = pl.BlockSpec(memory_space=pltpu.SMEM)
    return pl.pallas_call(
        body,
        out_shape=out_shape,
        in_specs=[smem] * len(scalars) + [vmem] * len(args),
        out_specs=jax.tree.map(lambda _: vmem, out_shape),
        scratch_shapes=list(scratch),
    )(*scalars, *args)


def shaped(shape, dtype):
    return jax.ShapeDtypeStruct(shape, dtype)


def selection(picks, slots):
    tokens = picks.shape[1]
    picked = jnp.broadcast_to(picks.astype(F32), (8, tokens)).astype(BF16)
    before = (iota((tokens, tokens), 0) < iota((tokens, tokens), 1)).astype(F32).astype(BF16)
    rank = dot(picked, before)[:1].astype(jnp.int32)
    hit = (iota((slots, tokens), 0) == rank) & (picks > 0)
    return hit.astype(F32).astype(BF16)


def pick_kernel(h_ref, c_ref, picks_ref, gain_ref, router_ref, send_ref, x_ref, cot_ref, inv_ref, gate_ref):
    lines, slots, width = send_ref.shape[0] // 2, send_ref.shape[1], send_ref.shape[2] // 2
    picks = picks_ref[...]
    sel = selection(picks, slots)
    x = dot(sel, h_ref[...])
    cot = dot(sel, c_ref[...])
    gate = 1.0 / (1.0 + jnp.exp(-jnp.sum(x * router_ref[...], axis=1, keepdims=True)))
    inv = lax.rsqrt(jnp.mean(x * x, axis=1, keepdims=True) + EPSILON)
    x_ref[...] = x.astype(BF16)
    cot_ref[...] = cot.astype(BF16)
    inv_ref[...] = inv
    gate_ref[...] = gate
    grads = (gate * cot).astype(BF16)
    normed = x * inv * gain_ref[...]
    normed = jnp.where(iota((slots, 1), 0) < jnp.sum(picks), normed, EMPTY).astype(BF16)
    for z in range(lines):
        cols = slice(z * width, (z + 1) * width)
        part = jnp.concatenate([normed[:, cols], grads[:, cols]], axis=1)
        send_ref[2 * z] = part
        send_ref[2 * z + 1] = part


def put(refs, at, value):
    if len(refs) == 1:
        refs[0][at] = value
        return
    for k, ref in enumerate(refs):

        @pl.when(at == k)
        def _(ref=ref):
            ref[...] = value


def weights_kernel(at_ref, wq_ref, wkv_ref, wo_ref, *outs, lines, cpd, kpd):
    z, p = at_ref[0], at_ref[1]
    to_plane, to_lines = outs[:PLANE], outs[PLANE:]
    width = wo_ref.shape[1] // lines
    for r in range(PLANE):
        places = [PLANE * k + r for k in range(lines)]
        columns = [wq_ref[:, i * cpd : (i + 1) * cpd] for i in places]
        columns += [wkv_ref[:, i * kpd : (i + 1) * kpd] for i in places]
        put(to_plane, p ^ r, jnp.concatenate(columns, axis=1))
    for k in range(lines):
        put(to_lines, z ^ k, wo_ref[:, k * width : (k + 1) * width])


def arrange_kernel(at_ref, *refs):
    z, p = at_ref[0], at_ref[1]
    wqkv_ref, wout_ref, cols_ref = refs[-3:]
    lines, _, width = wout_ref.shape
    fb = width // PLANE
    for r in range(PLANE):
        wqkv_ref[p ^ r] = refs[r][...]
    for k in range(lines):
        rows = refs[PLANE + k][...]
        wout_ref[z ^ k] = rows
        for r in range(PLANE):
            cols_ref[p ^ r, z ^ k] = rows[:, r * fb : (r + 1) * fb]


def columns_kernel(at_ref, *refs):
    out_ref = refs[-1]
    for r in range(PLANE):
        for k in range(refs[r].shape[0]):
            out_ref[PLANE * k + (at_ref[1] ^ r)] = refs[r][k]


def load_both(core, mine_ref, other_ref, all_ref):
    for i in range(mine_ref.shape[0]):
        all_ref[2 * i + core] = mine_ref[i]
        all_ref[2 * i + 1 - core] = other_ref[i]


def heads_kernel(at_ref, mine_ref, other_ref, wqkv_ref, wout_ref, *refs, rows, cpd, kpd, packed):
    core = at_ref[3]
    outs, got_ref = refs[:-1], refs[-1]
    part_ref, normed_ref, place_ref = outs[:3]
    lines = part_ref.shape[0]
    load_both(core, mine_ref, other_ref, got_ref)
    n, per, width = got_ref.shape
    slots = n * per
    half = width // 2
    fb = half // PLANE
    got = got_ref[...].reshape(slots, width)
    valid = got[:, :1].astype(F32) < EMPTY / 2
    ones = jnp.broadcast_to(jnp.where(valid, 1.0, 0.0), (slots, 128)).astype(BF16)
    earlier = (iota((slots, slots), 1) < iota((slots, slots), 0)).astype(F32).astype(BF16)
    rank = dot(earlier, ones)[:, :1].astype(jnp.int32)
    rank = jnp.where(valid, rank, -1)
    place = (rank == iota((slots, rows), 1)).astype(F32).astype(BF16)
    place_ref[...] = place
    compact = dot(place, got, 0, 0).astype(BF16)
    grads = compact[:, half:]
    for r in range(PLANE):
        normed_ref[r] = compact[:, r * fb : (r + 1) * fb]
    wqkv = wqkv_ref[...].reshape(half, lines * (cpd + kpd))
    query = dot(compact[:, :half], wqkv[:, : lines * cpd])
    kv = dot(wqkv[:, lines * cpd :], compact[:, :half], 0, 1)
    grad_heads = dot(grads, wout_ref[...].reshape(lines * cpd, half), 1, 1)
    top = rows // 2
    beside = lambda m: jnp.concatenate([m[:top], m[top:]], axis=1)
    for k in range(lines):
        q_part = query[:, k * cpd : (k + 1) * cpd]
        kv_part = kv[k * kpd : (k + 1) * kpd]
        g_part = grad_heads[:, k * cpd : (k + 1) * cpd]
        if packed:
            part_ref[k, :top] = beside(q_part)
            part_ref[k, top : top + kpd] = kv_part[:, :top]
            part_ref[k, top + kpd : top + 2 * kpd] = kv_part[:, top:]
            part_ref[k, top + 2 * kpd :] = beside(g_part)
        else:
            part_ref[k, :, :cpd] = q_part
            outs[3][k] = kv_part
            part_ref[k, :, cpd:] = g_part


def sum_kernel(part_ref, q_ref, g_ref):
    total = (part_ref[0] + part_ref[1] + (part_ref[2] + part_ref[3])).astype(BF16)
    lead = q_ref.shape[1]
    for i in range(q_ref.shape[0]):
        q_ref[i] = total[:lead]
        g_ref[i] = total[lead:]


def load_kv(q_all, kv_ref, kpd, top):
    n = q_all.shape[0]
    for i in range(n):
        kv_ref[i * kpd : (i + 1) * kpd, :top] = q_all[i, top : top + kpd]
        kv_ref[i * kpd : (i + 1) * kpd, top:] = q_all[i, top + kpd : top + 2 * kpd]


def probabilities(q, kt):
    top = q.shape[0]
    scale = HEAD_SIZE**-0.5

    def soft(scores, start):
        allowed = iota(scores.shape, 1) <= iota(scores.shape, 0) + start
        scores = jnp.where(allowed, scores * scale, -jnp.inf)
        e = jnp.exp(scores - jnp.max(scores, axis=1, keepdims=True))
        return e / jnp.sum(e, axis=1, keepdims=True)

    zero = jnp.zeros_like(kt)
    low = soft(dot(q, jnp.concatenate([kt[:, :top], zero[:, :top]], axis=0)), 0)
    return low, soft(dot(q, jnp.concatenate([zero, kt], axis=0)), top)


def forward_kernel(at_ref, *refs, packed, kpd):
    sources, (cols_ref, place_ref, send_ref, kv_out_ref) = refs[:2], refs[2:6]
    probs_refs = refs[6:-2]
    q_all, mixed_ref = refs[-2:]
    heads, top = q_all.shape[0], mixed_ref.shape[0] // 2
    if packed:
        load_both(at_ref[3], *sources, q_all)
        load_kv(q_all, kv_out_ref, kpd, top)
    else:
        q_all[...] = sources[0][...]
        kv_out_ref[...] = sources[1][...]

    def one_head(head, group):
        kt = kv_out_ref[pl.ds(group * HEAD_SIZE, HEAD_SIZE), :]
        vt = kv_out_ref[pl.ds((KEY_VALUE_HEADS + group) * HEAD_SIZE, HEAD_SIZE), :]
        low, high = probabilities(q_all[head, :top], kt)
        for ref, value in zip(probs_refs, (low, high)):
            ref[head] = value
        return dot(low.astype(BF16), vt[:, :top], 1, 1), dot(high.astype(BF16), vt, 1, 1)

    def pair(j):
        group = j // (GROUP // 2)
        low0, high0 = one_head(2 * j, group)
        low1, high1 = one_head(2 * j + 1, group)
        lanes = pl.ds(j * 2 * HEAD_SIZE, 2 * HEAD_SIZE)
        mixed_ref[:top, lanes] = jnp.concatenate([low0, low1], axis=1).astype(BF16)
        mixed_ref[top:, lanes] = jnp.concatenate([high0, high1], axis=1).astype(BF16)

    if packed:
        for j in range(heads // 2):
            pair(j)
    else:
        pl.loop(0, heads // 2)(pair)
    n, slots, _ = send_ref.shape
    out = dot(mixed_ref[...], cols_ref[...].reshape(Q_WIDTH, cols_ref.shape[2])).astype(BF16)
    spread = dot(place_ref[...], out).astype(BF16)
    for d in range(n):
        send_ref[d] = spread[d * slots : (d + 1) * slots]


def backward_kernel(at_ref, *refs, packed, kpd):
    count = 4 if packed else 2
    sources = refs[:count]
    kv_ref, wq_ref, wkv_ref, gain_ref, normed_ref, place_ref = refs[count : count + 6]
    probs_refs = refs[count + 6 : -6]
    up_ref, kvg_ref = refs[-6:-4]
    q_all, g_all, gq_ref, gkv_ref = refs[-4:]
    heads, top = q_all.shape[0], gq_ref.shape[0] // 2
    for source, all_ref in ((sources[: count // 2], q_all), (sources[count // 2 :], g_all)):
        if packed:
            load_both(at_ref[3], *source, all_ref)
        else:
            all_ref[...] = source[0][...]
    scale = HEAD_SIZE**-0.5
    gkv_ref[...] = jnp.zeros(gkv_ref.shape, F32)

    def one_head(head, group):
        keys = pl.ds(group * HEAD_SIZE, HEAD_SIZE)
        values = pl.ds((KEY_VALUE_HEADS + group) * HEAD_SIZE, HEAD_SIZE)
        kt, vt = kv_ref[keys, :], kv_ref[values, :]
        q, g = q_all[head, :top], g_all[head]
        zero = jnp.zeros_like(vt)

        def back(probs, gp):
            inner = jnp.sum(probs * gp, axis=1, keepdims=True)
            return (probs * (gp - inner)).astype(BF16)

        low, high = [ref[head] for ref in probs_refs] or probabilities(q, kt)
        gs_low = back(low, dot(g, jnp.concatenate([vt[:, :top], zero[:, :top]], axis=0)))
        gs_high = back(high, dot(g, jnp.concatenate([zero, vt], axis=0)))
        gkv_ref[keys, :] += dot(q, gs_high, 0, 0)[HEAD_SIZE:] * scale
        gkv_ref[keys, :top] += dot(q, gs_low, 0, 0)[:HEAD_SIZE] * scale
        gkv_ref[values, :] += dot(g, high.astype(BF16), 0, 0)[HEAD_SIZE:]
        gkv_ref[values, :top] += dot(g, low.astype(BF16), 0, 0)[:HEAD_SIZE]
        return dot(gs_low, kt[:, :top], 1, 1) * scale, dot(gs_high, kt, 1, 1) * scale

    def pair(j):
        group = j // (GROUP // 2)
        low0, high0 = one_head(2 * j, group)
        low1, high1 = one_head(2 * j + 1, group)
        lanes = pl.ds(j * 2 * HEAD_SIZE, 2 * HEAD_SIZE)
        gq_ref[:top, lanes] = jnp.concatenate([low0, low1], axis=1).astype(BF16)
        gq_ref[top:, lanes] = jnp.concatenate([high0, high1], axis=1).astype(BF16)

    if packed:
        for j in range(heads // 2):
            pair(j)
    else:
        pl.loop(0, heads // 2)(pair)
    n, slots, _ = up_ref.shape
    gkv = gkv_ref[...].astype(BF16)
    up = (dot(gq_ref[...], wq_ref[...], 1, 1) + dot(gkv, wkv_ref[...], 0, 1)) * gain_ref[at_ref[2]]
    kvg_ref[...] = dot(normed_ref[at_ref[1]], gkv, 0, 1)
    spread = dot(place_ref[...], up.astype(BF16)).astype(BF16)
    for d in range(n):
        up_ref[d] = spread[d * slots : (d + 1) * slots]


def mix_kernel(x_ref, cot_ref, gate_ref, got_ref, up_ref, send_ref, mixed_ref, logit_ref):
    n, slots, fb = up_ref.shape
    out = jnp.concatenate([got_ref[d] for d in range(n)], axis=1).astype(F32)
    x, gate = x_ref[...].astype(F32), gate_ref[...]
    mixed_ref[...] = (x + gate * out).astype(BF16)
    through = jnp.sum(cot_ref[...].astype(F32) * out, axis=1, keepdims=True)
    grad_logit = through * gate * (1.0 - gate)
    logit_ref[...] = grad_logit
    part = jnp.sum(grad_logit * x, axis=0, keepdims=True)
    row = iota((send_ref.shape[1] - slots, 1), 0)
    high = part.astype(BF16).astype(F32)
    middle = (part - high).astype(BF16).astype(F32)
    low = part - high - middle
    rows = jnp.where(row == 0, high, jnp.where(row == 1, middle, jnp.where(row == 2, low, 0.0))).astype(BF16)
    for d in range(n):
        send_ref[d, :slots] = up_ref[d]
        send_ref[d, slots:] = rows[:, d * fb : (d + 1) * fb]


def place_rows(picks, rows, tokens):
    sel = selection(picks, rows.shape[0])
    taken = dot(sel, jnp.ones((rows.shape[0], 128), BF16), 0, 0)[:, :1] > 0.5
    return jnp.where(taken, dot(sel, rows, 0, 0), tokens.astype(F32)).astype(BF16)


def tokens_kernel(h_ref, picks_ref, mixed_ref, out_ref):
    out_ref[...] = place_rows(picks_ref[...], mixed_ref[...], h_ref[...])


def add_kernel(a_ref, b_ref, out_ref):
    out_ref[...] = a_ref[...] + b_ref[...]


def finish_kernel(c_ref, picks_ref, router_ref, logit_ref, x_ref, cot_ref, inv_ref, got_ref, grad_ref):
    n = got_ref.shape[0]
    slots = x_ref.shape[0]
    up = jnp.concatenate([got_ref[d, :slots] for d in range(n)], axis=1).astype(F32)
    x, inv = x_ref[...].astype(F32), inv_ref[...]
    grad_block = inv * up - x * inv**3 * jnp.mean(up * x, axis=1, keepdims=True)
    grad_block = grad_block.astype(BF16).astype(F32)
    rows = (cot_ref[...].astype(F32) + logit_ref[...] * router_ref[...] + grad_block).astype(BF16)
    grad_ref[...] = place_rows(picks_ref[...], rows, c_ref[...])


def exchange(x, axes):
    return lax.all_to_all(x, axes, 0, 0, tiled=True)


def swap(x, n, bit):
    return lax.ppermute(x, SEQ, [(i, i ^ bit) for i in range(n)])


def block(hidden, cotangent, picks, gain, router, w_query, w_kv, w_out):
    lines = lax.axis_size("zz")
    n = lines * PLANE
    dp = lax.axis_size("dp")
    z, core = lax.axis_index("zz"), lax.axis_index("cc")
    p = 2 * lax.axis_index("yy") + core
    me = PLANE * z + p
    where = jnp.stack([z, p, me, core]).astype(jnp.int32)
    hidden, cotangent = hidden[0], cotangent[0]
    tokens = hidden.shape[0]
    slots = tokens // 4
    rows = n * (tokens // 8)
    top = rows // 2
    fb = MODEL_WIDTH // n
    cpd = Q_WIDTH // n
    kpd = KV_WIDTH // n
    packed = cpd == HEAD_SIZE
    as_row = lambda v: v.reshape(1, -1)

    lines_apart = lines <= 4
    to_plane = [shaped((fb, lines * (cpd + kpd)), BF16)] * PLANE
    to_lines = [shaped((cpd, PLANE * fb), BF16)] * lines if lines_apart else [shaped((lines, cpd, PLANE * fb), BF16)]
    out = call(
        functools.partial(weights_kernel, lines=lines, cpd=cpd, kpd=kpd),
        tuple(to_plane + to_lines),
        w_query,
        w_kv,
        w_out,
        scalars=(where,),
    )
    to_plane, to_lines = out[:PLANE], out[PLANE:]
    if not lines_apart:
        to_lines = [to_lines[0][k] for k in range(lines)]
    wqkv = [to_plane[0]] + [swap(to_plane[r], n, r) for r in range(1, PLANE)]
    wout = [to_lines[0]] + [swap(to_lines[k], n, PLANE * k) for k in range(1, lines)]
    wqkv, wout, cols = call(
        arrange_kernel,
        (
            shaped((PLANE, fb, lines * (cpd + kpd)), BF16),
            shaped((lines, cpd, PLANE * fb), BF16),
            shaped((PLANE, lines, cpd, fb), BF16),
        ),
        *wqkv,
        *wout,
        scalars=(where,),
    )

    send, x, cot, inv, gate = call(
        pick_kernel,
        (
            shaped((2 * lines, slots, 2 * PLANE * fb), BF16),
            shaped((slots, MODEL_WIDTH), BF16),
            shaped((slots, MODEL_WIDTH), BF16),
            shaped((slots, 1), F32),
            shaped((slots, 1), F32),
        ),
        hidden,
        cotangent,
        picks,
        as_row(gain),
        as_row(router),
    )
    mine = exchange(send, LINES)
    other = swap(mine, n, 1)

    part = (lines, top + 2 * kpd + top, 2 * cpd) if packed else (lines, rows, 2 * cpd)
    outs = [
        shaped(part, F32),
        shaped((PLANE, rows, fb), BF16),
        shaped((n * slots, rows), BF16),
    ]
    if not packed:
        outs += [shaped((lines, kpd, rows), F32)]
    part, normed, place, *kv_part = call(
        functools.partial(heads_kernel, rows=rows, cpd=cpd, kpd=kpd, packed=packed),
        tuple(outs),
        mine,
        other,
        wqkv,
        wout,
        scalars=(where,),
        scratch=(pltpu.VMEM((n, slots, 2 * PLANE * fb), BF16),),
    )
    cols = [cols[0]] + [swap(cols[r], n, r) for r in range(1, PLANE)]
    cols = call(columns_kernel, shaped((n, cpd, fb), BF16), *cols, scalars=(where,))
    part = exchange(part, "zz")
    if packed:
        lead = top + 2 * kpd
        q_pack, g_pack = call(
            sum_kernel, (shaped((2 * lines, lead, 2 * cpd), BF16), shaped((2 * lines, top, 2 * cpd), BF16)), part
        )
        q_refs = exchange(q_pack, LINES)
        q_refs = (q_refs, swap(q_refs, n, 1))
        g_refs = exchange(g_pack, LINES)
        g_refs = (g_refs, swap(g_refs, n, 1))
        kv_refs = ()
    else:
        per = HEAD_SIZE // cpd
        everything = jnp.sum(part, axis=0).astype(BF16)
        everything = lax.all_gather(everything, SEQ, axis=0).reshape(QUERY_HEADS, per, 2, top, 2, cpd)
        everything = everything.transpose(4, 0, 3, 2, 1, 5).reshape(2, QUERY_HEADS, top, 2 * HEAD_SIZE)
        q_refs, g_refs = (everything[0],), (everything[1],)
        kv_part = jnp.sum(lax.all_to_all(kv_part[0], "zz", 0, 0, tiled=True), axis=0).astype(BF16)
        kv_refs = (lax.all_gather(kv_part, SEQ, axis=0, tiled=True),)
    q_scratch = pltpu.VMEM((QUERY_HEADS, top + (2 * kpd if packed else 0), 2 * HEAD_SIZE), BF16)

    probs = (shaped((QUERY_HEADS, top, top), F32), shaped((QUERY_HEADS, top, rows), F32)) if packed else ()
    send, kv_all, *probs = call(
        functools.partial(forward_kernel, packed=packed, kpd=kpd),
        (
            shaped((n, slots, fb), BF16),
            shaped((KV_WIDTH, rows), BF16),
            *probs,
        ),
        *q_refs,
        *kv_refs,
        cols,
        place,
        scalars=(where,),
        scratch=(q_scratch, pltpu.VMEM((rows, Q_WIDTH), BF16)),
    )
    got = exchange(send, SEQ)
    up, kv_part = call(
        functools.partial(backward_kernel, packed=packed, kpd=kpd),
        (shaped((n, slots, fb), BF16), shaped((fb, KV_WIDTH), F32)),
        *q_refs,
        *g_refs,
        kv_all,
        w_query,
        w_kv,
        gain.reshape(n, 1, fb),
        normed,
        place,
        *probs,
        scalars=(where,),
        scratch=(
            q_scratch,
            pltpu.VMEM((QUERY_HEADS, top, 2 * HEAD_SIZE), BF16),
            pltpu.VMEM((rows, Q_WIDTH), BF16),
            pltpu.VMEM((KV_WIDTH, rows), F32),
        ),
    )
    send, mixed_rows, grad_logit = call(
        mix_kernel,
        (
            shaped((n, slots + 16, fb), BF16),
            shaped((slots, MODEL_WIDTH), BF16),
            shaped((slots, 1), F32),
        ),
        x,
        cot,
        gate,
        got,
        up,
    )
    got = exchange(send, SEQ)
    mixed = call(tokens_kernel, shaped((tokens, MODEL_WIDTH), BF16), hidden, picks, mixed_rows)

    def add_over_dp(v):
        if dp != 2:
            return lax.psum(v, "dp")
        other = lax.ppermute(v, "dp", [(0, 1), (1, 0)])
        return call(add_kernel, shaped(v.shape, F32), v, other)

    kv_grad = add_over_dp(kv_part)
    router_grad = jnp.sum(got[:, slots : slots + 3].astype(F32), axis=(0, 1)).reshape(1, fb)
    router_grad = add_over_dp(router_grad).reshape(fb)
    input_grad = call(
        finish_kernel,
        shaped((tokens, MODEL_WIDTH), BF16),
        cotangent,
        picks,
        as_row(router),
        grad_logit,
        x,
        cot,
        inv,
        got,
    )
    return mixed[None], input_grad[None], kv_grad, router_grad


def solution(mesh):
    dp, n = mesh.shape["dp"], mesh.shape["seq"]
    split = Mesh(mesh.devices.reshape(dp, n // PLANE, PLANE // 2, 2), ("dp",) + SEQ)
    rows = P("dp", SEQ, None)
    return jax.shard_map(
        block,
        mesh=split,
        in_specs=(rows, rows, P("dp", SEQ), P(), P(), P(SEQ, None), P(SEQ, None), P(SEQ, None)),
        out_specs=(rows, rows, P(SEQ, None), P(SEQ)),
        check_vma=False,
    )
```

```python
import functools

import jax
import jax.numpy as jnp
from jax import lax
from jax.experimental import pallas as pl
from jax.experimental.pallas import tpu as pltpu
from jax.sharding import Mesh, PartitionSpec as P


MODEL_WIDTH = 2048
QUERY_HEADS = 16
KEY_VALUE_HEADS = 2
HEAD_SIZE = 64
GROUP = QUERY_HEADS // KEY_VALUE_HEADS
KV_WIDTH = 2 * KEY_VALUE_HEADS * HEAD_SIZE
Q_WIDTH = QUERY_HEADS * HEAD_SIZE
EPSILON = 1e-05
PLANE = 4
LANES = 128
LINES = ("zz", "yy")
SEQ = LINES + ("cc",)

F32 = jnp.float32
BF16 = jnp.bfloat16


def dot(a, b, ca=1, cb=0, precision=None):
    return lax.dot_general(a, b, (((ca,), (cb,)), ((), ())), precision=precision, preferred_element_type=F32)


def pieces(v):
    high = v.astype(BF16).astype(F32)
    middle = (v - high).astype(BF16).astype(F32)
    return high, middle, v - high - middle


def iota(shape, dim):
    return lax.broadcasted_iota(jnp.int32, shape, dim)


def call(body, out_shape, *args, scalars=(), scratch=()):
    vmem = pl.BlockSpec(memory_space=pltpu.VMEM)
    smem = pl.BlockSpec(memory_space=pltpu.SMEM)
    return pl.pallas_call(
        body,
        out_shape=out_shape,
        in_specs=[smem] * len(scalars) + [vmem] * len(args),
        out_specs=jax.tree.map(lambda _: vmem, out_shape),
        scratch_shapes=list(scratch),
    )(*scalars, *args)


def shaped(shape, dtype):
    return jax.ShapeDtypeStruct(shape, dtype)


def selection(picks, slots):
    tokens = picks.shape[1]
    picked = jnp.broadcast_to(picks.astype(F32), (8, tokens)).astype(BF16)
    before = (iota((tokens, tokens), 0) < iota((tokens, tokens), 1)).astype(F32).astype(BF16)
    rank = dot(picked, before)[:1].astype(jnp.int32)
    hit = (iota((slots, tokens), 0) == rank) & (picks > 0)
    return hit.astype(F32).astype(BF16)


def pick_kernel(h_ref, c_ref, picks_ref, router_ref, send_ref, x_ref, cot_ref, inv_ref, gate_ref):
    lines, slots = send_ref.shape[0] // 2, send_ref.shape[1]
    width = MODEL_WIDTH // lines
    picks = picks_ref[...]
    sel = selection(picks, slots)
    x = dot(sel, h_ref[...])
    cot = dot(sel, c_ref[...])
    gate = 1.0 / (1.0 + jnp.exp(-jnp.sum(x * router_ref[...], axis=1, keepdims=True)))
    inv = lax.rsqrt(jnp.mean(x * x, axis=1, keepdims=True) + EPSILON)
    inv_ref[...] = inv
    gate_ref[...] = gate
    lane = iota((slots, LANES), 1)
    extra = jnp.where((lane == 6) & (iota((slots, 1), 0) < jnp.sum(picks)), 1.0, 0.0)
    for k, piece in enumerate(pieces(gate) + pieces(inv)):
        extra = jnp.where(lane == k, piece, extra)
    extra = extra.astype(BF16)
    x, cot = x.astype(BF16), cot.astype(BF16)
    x_ref[...] = x
    cot_ref[...] = cot
    for z in range(lines):
        cols = slice(z * width, (z + 1) * width)
        part = jnp.concatenate([x[:, cols], cot[:, cols], extra], axis=1)
        send_ref[2 * z] = part
        send_ref[2 * z + 1] = part


def put(refs, at, value):
    if len(refs) == 1:
        refs[0][at] = value
        return
    for k, ref in enumerate(refs):

        @pl.when(at == k)
        def _(ref=ref):
            ref[...] = value


def weights_kernel(at_ref, wq_ref, wkv_ref, wo_ref, *outs, lines, cpd, kpd):
    z, p = at_ref[0], at_ref[1]
    to_plane, to_lines = outs[:PLANE], outs[PLANE:]
    width = wo_ref.shape[1] // lines
    for r in range(PLANE):
        places = [PLANE * k + r for k in range(lines)]
        columns = [wq_ref[:, i * cpd : (i + 1) * cpd] for i in places]
        columns += [wkv_ref[:, i * kpd : (i + 1) * kpd] for i in places]
        put(to_plane, p ^ r, jnp.concatenate(columns, axis=1))
    for k in range(lines):
        put(to_lines, z ^ k, wo_ref[:, k * width : (k + 1) * width])


def arrange_kernel(at_ref, *refs):
    z, p = at_ref[0], at_ref[1]
    wqkv_ref, wout_ref, cols_ref = refs[-3:]
    lines, _, width = wout_ref.shape
    fb = width // PLANE
    for r in range(PLANE):
        wqkv_ref[p ^ r] = refs[r][...]
    for k in range(lines):
        rows = refs[PLANE + k][...]
        wout_ref[z ^ k] = rows
        for r in range(PLANE):
            cols_ref[p ^ r, z ^ k] = rows[:, r * fb : (r + 1) * fb]


def columns_kernel(at_ref, *refs):
    out_ref = refs[-1]
    for r in range(PLANE):
        for k in range(refs[r].shape[0]):
            out_ref[PLANE * k + (at_ref[1] ^ r)] = refs[r][k]


def load_both(core, mine_ref, other_ref, all_ref):
    for i in range(mine_ref.shape[0]):
        all_ref[2 * i + core] = mine_ref[i]
        all_ref[2 * i + 1 - core] = other_ref[i]


def heads_kernel(at_ref, mine_ref, other_ref, wqkv_ref, wout_ref, gain_ref, *refs, rows, cpd, kpd, packed):
    core = at_ref[3]
    outs, got_ref = refs[:-1], refs[-1]
    part_ref, place_ref, gate_ref, normed_ref, x_ref, cot_ref = outs[:6]
    lines = part_ref.shape[0]
    load_both(core, mine_ref, other_ref, got_ref)
    n, per, width = got_ref.shape
    slots = n * per
    half = (width - LANES) // 2
    fb = half // PLANE
    got = got_ref[...].reshape(slots, width)
    valid = got[:, 2 * half + 6 : 2 * half + 7].astype(F32) > 0.5
    ones = jnp.broadcast_to(jnp.where(valid, 1.0, 0.0), (slots, 128)).astype(BF16)
    earlier = (iota((slots, slots), 1) < iota((slots, slots), 0)).astype(F32).astype(BF16)
    rank = dot(earlier, ones)[:, :1].astype(jnp.int32)
    rank = jnp.where(valid, rank, -1)
    place = (rank == iota((slots, rows), 1)).astype(F32).astype(BF16)
    place_ref[...] = place
    compact = dot(place, got, 0, 0)
    extra = compact[:, 2 * half :]
    x, cot = compact[:, :half], compact[:, half : 2 * half]
    add_up = lambda k: extra[:, k : k + 1] + extra[:, k + 1 : k + 2] + extra[:, k + 2 : k + 3]
    gate, inv = add_up(0), add_up(3)
    normed = (x * inv * gain_ref[at_ref[0]]).astype(BF16)
    grads = (gate * cot).astype(BF16)
    three = jnp.where(iota((8, LANES), 1) < 3, 1.0, 0.0).astype(BF16)
    gate_ref[...] = dot(three, extra.astype(BF16), 1, 1)
    for r in range(PLANE):
        cols = slice(r * fb, (r + 1) * fb)

        @pl.when(at_ref[1] == r)
        def _(cols=cols):
            normed_ref[...] = normed[:, cols]
            x_ref[...] = x[:, cols].astype(BF16)
            cot_ref[...] = cot[:, cols].astype(BF16)

    wqkv = wqkv_ref[...].reshape(half, lines * (cpd + kpd))
    query = dot(normed, wqkv[:, : lines * cpd])
    kv = dot(wqkv[:, lines * cpd :], normed, 0, 1)
    grad_heads = dot(grads, wout_ref[...].reshape(lines * cpd, half), 1, 1)
    top = rows // 2
    beside = lambda m: jnp.concatenate([m[:top], m[top:]], axis=1)
    for k in range(lines):
        q_part = query[:, k * cpd : (k + 1) * cpd]
        kv_part = kv[k * kpd : (k + 1) * kpd]
        g_part = grad_heads[:, k * cpd : (k + 1) * cpd]
        if packed:
            part_ref[k, :top] = beside(q_part)
            part_ref[k, top : top + kpd] = kv_part[:, :top]
            part_ref[k, top + kpd : top + 2 * kpd] = kv_part[:, top:]
            part_ref[k, top + 2 * kpd :] = beside(g_part)
        else:
            part_ref[k, :, :cpd] = q_part
            outs[6][k] = kv_part
            part_ref[k, :, cpd:] = g_part


def sum_kernel(part_ref, q_ref, g_ref):
    total = sum(part_ref[k] for k in range(part_ref.shape[0])).astype(BF16)
    lead = q_ref.shape[1]
    for i in range(q_ref.shape[0]):
        q_ref[i] = total[:lead]
        g_ref[i] = total[lead:]


def load_kv(q_all, kv_ref, kpd, top):
    n = q_all.shape[0]
    for i in range(n):
        kv_ref[i * kpd : (i + 1) * kpd, :top] = q_all[i, top : top + kpd]
        kv_ref[i * kpd : (i + 1) * kpd, top:] = q_all[i, top + kpd : top + 2 * kpd]


def probabilities(q, kt):
    heads, top, lanes = q.shape
    scale = HEAD_SIZE**-0.5

    def soft(padded, start):
        scores = dot(q.reshape(heads * top, lanes), padded).reshape(heads, top, padded.shape[1])
        allowed = iota(scores.shape, 2) <= iota(scores.shape, 1) + start
        scores = jnp.where(allowed, scores * scale, -jnp.inf)
        e = jnp.exp(scores - jnp.max(scores, axis=2, keepdims=True))
        return e / jnp.sum(e, axis=2, keepdims=True)

    zero = jnp.zeros_like(kt)
    low = soft(jnp.concatenate([kt[:, :top], zero[:, :top]], axis=0), 0)
    return low, soft(jnp.concatenate([zero, kt], axis=0), top)


def flat(x):
    return x.reshape(x.shape[0] * x.shape[1], x.shape[2])


def by_lanes(ref, first, low, high):
    top = ref.shape[0] // 2
    for start, part in ((0, low), (top, high)):
        for i in range(0, part.shape[0] // top, 2):
            both = [part[(i + j) * top : (i + j + 1) * top] for j in range(2)]
            lanes = pl.ds(pl.multiple_of((first + i) * HEAD_SIZE, 2 * HEAD_SIZE), 2 * HEAD_SIZE)
            ref[start : start + top, lanes] = jnp.concatenate(both, axis=1).astype(BF16)


def over_heads(body, heads, packed):
    if packed:
        for group in range(KEY_VALUE_HEADS):
            body(group * GROUP, GROUP, group)
    else:

        @pl.loop(0, heads // 2)
        def _(j):
            body(2 * j, 2, j // (GROUP // 2))


def forward_kernel(at_ref, *refs, packed, kpd):
    sources, (cols_ref, place_ref, cot_ref, send_ref, kv_out_ref, through_ref) = refs[:2], refs[2:8]
    probs_refs = refs[8:-2]
    q_all, mixed_ref = refs[-2:]
    heads, top = q_all.shape[0], mixed_ref.shape[0] // 2
    if packed:
        load_both(at_ref[3], *sources, q_all)
        load_kv(q_all, kv_out_ref, kpd, top)
    else:
        q_all[...] = sources[0][...]
        kv_out_ref[...] = sources[1][...]

    def some_heads(first, count, group):
        kt = kv_out_ref[pl.ds(group * HEAD_SIZE, HEAD_SIZE), :]
        vt = kv_out_ref[pl.ds((KEY_VALUE_HEADS + group) * HEAD_SIZE, HEAD_SIZE), :]
        low, high = probabilities(q_all[pl.ds(first, count), :top], kt)
        for ref, value in zip(probs_refs, (low, high)):
            ref[pl.ds(first, count)] = value
        low, high = flat(low).astype(BF16), flat(high).astype(BF16)
        by_lanes(mixed_ref, first, dot(low, vt[:, :top], 1, 1), dot(high, vt, 1, 1))

    over_heads(some_heads, heads, packed)
    n, slots, _ = send_ref.shape
    out = dot(mixed_ref[...], cols_ref[...].reshape(Q_WIDTH, cols_ref.shape[2])).astype(BF16)
    terms = cot_ref[...].astype(F32) * out.astype(F32)
    through_ref[...] = dot(jnp.ones((8, terms.shape[1]), F32), terms, 1, 1, lax.Precision.HIGHEST)
    spread = dot(place_ref[...], out).astype(BF16)
    for d in range(n):
        send_ref[d] = spread[d * slots : (d + 1) * slots]


def backward_kernel(at_ref, *refs, packed, kpd):
    count = 4 if packed else 2
    sources = refs[:count]
    kv_ref, wq_ref, wkv_ref, gain_ref, normed_ref, place_ref, out_ref = refs[count : count + 7]
    probs_refs = refs[count + 7 : -6]
    send_ref, kv_grad_ref = refs[-6:-4]
    q_all, g_all, gq_ref, gkv_ref = refs[-4:]
    heads, top = q_all.shape[0], gq_ref.shape[0] // 2
    for source, all_ref in ((sources[: count // 2], q_all), (sources[count // 2 :], g_all)):
        if packed:
            load_both(at_ref[3], *source, all_ref)
        else:
            all_ref[...] = source[0][...]
    scale = HEAD_SIZE**-0.5
    gkv_ref[...] = jnp.zeros(gkv_ref.shape, F32)

    def some_heads(first, count, group):
        some = pl.ds(first, count)
        keys = pl.ds(group * HEAD_SIZE, HEAD_SIZE)
        values = pl.ds((KEY_VALUE_HEADS + group) * HEAD_SIZE, HEAD_SIZE)
        kt, vt = kv_ref[keys, :], kv_ref[values, :]
        q, g = q_all[some, :top], flat(g_all[some])
        low, high = [ref[some] for ref in probs_refs] or probabilities(q, kt)
        q = flat(q)
        zero = jnp.zeros_like(vt)

        def back(probs, padded):
            gp = dot(g, padded).reshape(probs.shape)
            inner = jnp.sum(probs * gp, axis=2, keepdims=True)
            return flat((probs * (gp - inner)).astype(BF16))

        gs_low = back(low, jnp.concatenate([vt[:, :top], zero[:, :top]], axis=0))
        gs_high = back(high, jnp.concatenate([zero, vt], axis=0))
        low, high = flat(low).astype(BF16), flat(high).astype(BF16)
        gkv_ref[keys, :] += dot(q, gs_high, 0, 0)[HEAD_SIZE:] * scale
        gkv_ref[keys, :top] += dot(q, gs_low, 0, 0)[:HEAD_SIZE] * scale
        gkv_ref[values, :] += dot(g, high, 0, 0)[HEAD_SIZE:]
        gkv_ref[values, :top] += dot(g, low, 0, 0)[:HEAD_SIZE]
        by_lanes(gq_ref, first, dot(gs_low, kt[:, :top], 1, 1) * scale, dot(gs_high, kt, 1, 1) * scale)

    over_heads(some_heads, heads, packed)
    n, slots, fb = out_ref.shape
    gkv = gkv_ref[...].astype(BF16)
    up = (dot(gq_ref[...], wq_ref[...], 1, 1) + dot(gkv, wkv_ref[...], 0, 1)) * gain_ref[at_ref[2]]
    spread = dot(place_ref[...], up.astype(BF16)).astype(BF16)
    for d in range(n):
        send_ref[d, :, :fb] = out_ref[d]
        send_ref[d, :, fb:] = spread[d * slots : (d + 1) * slots]
    kv_grad_ref[...] = dot(normed_ref[...], gkv, 0, 1)


def router_kernel(x_ref, gate_ref, *refs):
    gate, out_ref = gate_ref[...], refs[-1]
    grad_logit = sum(ref[...] for ref in refs[:-1]) * gate * (1.0 - gate)
    out_ref[...] = dot(grad_logit, x_ref[...].astype(F32), 1, 0, lax.Precision.HIGHEST)


def place_rows(picks, rows, tokens):
    sel = selection(picks, rows.shape[0])
    taken = dot(sel, jnp.ones((rows.shape[0], 128), BF16), 0, 0)[:, :1] > 0.5
    return jnp.where(taken, dot(sel, rows, 0, 0), tokens.astype(F32)).astype(BF16)


def add_kernel(a_ref, b_ref, out_ref):
    out_ref[...] = a_ref[...] + b_ref[...]


def finish_kernel(
    h_ref, c_ref, picks_ref, router_ref, gate_ref, x_ref, cot_ref, inv_ref, got_ref, part_ref, other_ref,
    mixed_ref, grad_ref, router_grad_ref
):
    router_grad_ref[...] = part_ref[:1] + other_ref[:1]
    n, _, width = got_ref.shape
    fb = width // 2
    take = lambda k: jnp.concatenate([got_ref[d, :, k * fb : (k + 1) * fb] for d in range(n)], axis=1).astype(F32)
    out, up = take(0), take(1)
    x, inv, gate = x_ref[...].astype(F32), inv_ref[...], gate_ref[...]
    picks = picks_ref[...]
    mixed_ref[...] = place_rows(picks, (x + gate * out).astype(BF16), h_ref[...])
    cot = cot_ref[...].astype(F32)
    grad_logit = jnp.sum(cot * out, axis=1, keepdims=True) * gate * (1.0 - gate)
    grad_block = inv * up - x * inv**3 * jnp.mean(up * x, axis=1, keepdims=True)
    grad_block = grad_block.astype(BF16).astype(F32)
    rows = (cot + grad_logit * router_ref[...] + grad_block).astype(BF16)
    grad_ref[...] = place_rows(picks, rows, c_ref[...])


def exchange(x, axes):
    return lax.all_to_all(x, axes, 0, 0, tiled=True)


def swap(x, n, bit):
    return lax.ppermute(x, SEQ, [(i, i ^ bit) for i in range(n)])


def block(hidden, cotangent, picks, gain, router, w_query, w_kv, w_out):
    lines = lax.axis_size("zz")
    n = lines * PLANE
    dp = lax.axis_size("dp")
    z, core = lax.axis_index("zz"), lax.axis_index("cc")
    p = 2 * lax.axis_index("yy") + core
    me = PLANE * z + p
    where = jnp.stack([z, p, me, core]).astype(jnp.int32)
    hidden, cotangent = hidden[0], cotangent[0]
    tokens = hidden.shape[0]
    slots = tokens // 4
    rows = n * (tokens // 8)
    top = rows // 2
    fb = MODEL_WIDTH // n
    cpd = Q_WIDTH // n
    kpd = KV_WIDTH // n
    packed = cpd == HEAD_SIZE
    as_row = lambda v: v.reshape(1, -1)

    lines_apart = lines <= 4
    to_plane = [shaped((fb, lines * (cpd + kpd)), BF16)] * PLANE
    to_lines = [shaped((cpd, PLANE * fb), BF16)] * lines if lines_apart else [shaped((lines, cpd, PLANE * fb), BF16)]
    out = call(
        functools.partial(weights_kernel, lines=lines, cpd=cpd, kpd=kpd),
        tuple(to_plane + to_lines),
        w_query,
        w_kv,
        w_out,
        scalars=(where,),
    )
    to_plane, to_lines = out[:PLANE], out[PLANE:]
    if not lines_apart:
        to_lines = [to_lines[0][k] for k in range(lines)]
    wqkv = [to_plane[0]] + [swap(to_plane[r], n, r) for r in range(1, PLANE)]
    wout = [to_lines[0]] + [swap(to_lines[k], n, PLANE * k) for k in range(1, lines)]
    wqkv, wout, cols = call(
        arrange_kernel,
        (
            shaped((PLANE, fb, lines * (cpd + kpd)), BF16),
            shaped((lines, cpd, PLANE * fb), BF16),
            shaped((PLANE, lines, cpd, fb), BF16),
        ),
        *wqkv,
        *wout,
        scalars=(where,),
    )

    send, x, cot, inv, gate = call(
        pick_kernel,
        (
            shaped((2 * lines, slots, 2 * PLANE * fb + LANES), BF16),
            shaped((slots, MODEL_WIDTH), BF16),
            shaped((slots, MODEL_WIDTH), BF16),
            shaped((slots, 1), F32),
            shaped((slots, 1), F32),
        ),
        hidden,
        cotangent,
        picks,
        as_row(router),
    )
    mine = exchange(send, LINES)
    other = swap(mine, n, 1)

    part = (lines, top + 2 * kpd + top, 2 * cpd) if packed else (lines, rows, 2 * cpd)
    outs = [
        shaped(part, F32),
        shaped((n * slots, rows), BF16),
        shaped((8, rows), F32),
    ]
    outs += [shaped((rows, fb), BF16)] * 3
    if not packed:
        outs += [shaped((lines, kpd, rows), F32)]
    part, place, gate_rows, normed, own_x, own_cot, *kv_part = call(
        functools.partial(heads_kernel, rows=rows, cpd=cpd, kpd=kpd, packed=packed),
        tuple(outs),
        mine,
        other,
        wqkv,
        wout,
        gain.reshape(lines, 1, PLANE * fb),
        scalars=(where,),
        scratch=(pltpu.VMEM((n, slots, 2 * PLANE * fb + LANES), BF16),),
    )
    cols = [cols[0]] + [swap(cols[r], n, r) for r in range(1, PLANE)]
    cols = call(columns_kernel, shaped((n, cpd, fb), BF16), *cols, scalars=(where,))
    part = exchange(part, "zz")
    if packed:
        lead = top + 2 * kpd
        q_pack, g_pack = call(
            sum_kernel, (shaped((2 * lines, lead, 2 * cpd), BF16), shaped((2 * lines, top, 2 * cpd), BF16)), part
        )
        q_refs = exchange(q_pack, LINES)
        q_refs = (q_refs, swap(q_refs, n, 1))
        g_refs = exchange(g_pack, LINES)
        g_refs = (g_refs, swap(g_refs, n, 1))
        kv_refs = ()
    else:
        per = HEAD_SIZE // cpd
        everything = jnp.sum(part, axis=0).astype(BF16)
        everything = lax.all_gather(everything, SEQ, axis=0).reshape(QUERY_HEADS, per, 2, top, 2, cpd)
        everything = everything.transpose(4, 0, 3, 2, 1, 5).reshape(2, QUERY_HEADS, top, 2 * HEAD_SIZE)
        q_refs, g_refs = (everything[0],), (everything[1],)
        kv_part = lax.all_to_all(kv_part[0], "zz", 0, 0, tiled=True)
        kv_part = jnp.sum(kv_part, axis=0).astype(BF16)
        kv_refs = (lax.all_gather(kv_part, SEQ, axis=0, tiled=True),)
    q_scratch = pltpu.VMEM((QUERY_HEADS, top + (2 * kpd if packed else 0), 2 * HEAD_SIZE), BF16)

    probs = (shaped((QUERY_HEADS, top, top), F32), shaped((QUERY_HEADS, top, rows), F32)) if packed else ()
    out, kv_all, through, *probs = call(
        functools.partial(forward_kernel, packed=packed, kpd=kpd),
        (
            shaped((n, slots, fb), BF16),
            shaped((KV_WIDTH, rows), BF16),
            shaped((8, rows), F32),
            *probs,
        ),
        *q_refs,
        *kv_refs,
        cols,
        place,
        own_cot,
        scalars=(where,),
        scratch=(q_scratch, pltpu.VMEM((rows, Q_WIDTH), BF16)),
    )
    through = [through] + [swap(through, n, r) for r in range(1, PLANE)]
    send, kv_part = call(
        functools.partial(backward_kernel, packed=packed, kpd=kpd),
        (shaped((n, slots, 2 * fb), BF16), shaped((fb, KV_WIDTH), F32)),
        *q_refs,
        *g_refs,
        kv_all,
        w_query,
        w_kv,
        gain.reshape(n, 1, fb),
        normed,
        place,
        out,
        *probs,
        scalars=(where,),
        scratch=(
            q_scratch,
            pltpu.VMEM((QUERY_HEADS, top, 2 * HEAD_SIZE), BF16),
            pltpu.VMEM((rows, Q_WIDTH), BF16),
            pltpu.VMEM((KV_WIDTH, rows), F32),
        ),
    )
    got = exchange(send, SEQ)
    through = sum(through[1:], through[0])
    through = [through] + [swap(through, n, PLANE * k) for k in range(1, lines)]
    router_part = call(router_kernel, shaped((8, fb), F32), own_x, gate_rows, *through)
    if dp == 2:
        pair = [(0, 1), (1, 0)]
        other = lax.ppermute(kv_part, "dp", pair)
        kv_grad = call(add_kernel, shaped((fb, KV_WIDTH), F32), kv_part, other)
        router_other = lax.ppermute(router_part, "dp", pair)
    else:
        kv_grad, router_part = lax.psum(kv_part, "dp"), lax.psum(router_part, "dp")
        router_other = jnp.zeros_like(router_part)
    mixed, input_grad, router_grad = call(
        finish_kernel,
        (
            shaped((tokens, MODEL_WIDTH), BF16),
            shaped((tokens, MODEL_WIDTH), BF16),
            shaped((1, fb), F32),
        ),
        hidden,
        cotangent,
        picks,
        as_row(router),
        gate,
        x,
        cot,
        inv,
        got,
        router_part,
        router_other,
    )
    return mixed[None], input_grad[None], kv_grad, router_grad.reshape(fb)


def solution(mesh):
    dp, n = mesh.shape["dp"], mesh.shape["seq"]
    split = Mesh(mesh.devices.reshape(dp, n // PLANE, PLANE // 2, 2), ("dp",) + SEQ)
    rows = P("dp", SEQ, None)
    return jax.shard_map(
        block,
        mesh=split,
        in_specs=(rows, rows, P("dp", SEQ), P(), P(), P(SEQ, None), P(SEQ, None), P(SEQ, None)),
        out_specs=(rows, rows, P(SEQ, None), P(SEQ)),
        check_vma=False,
    )
```

```python
import functools

import jax
import jax.numpy as jnp
from jax import lax
from jax.experimental import pallas as pl
from jax.experimental.pallas import tpu as pltpu
from jax.sharding import Mesh, PartitionSpec as P


MODEL_WIDTH = 2048
QUERY_HEADS = 16
KEY_VALUE_HEADS = 2
HEAD_SIZE = 64
GROUP = QUERY_HEADS // KEY_VALUE_HEADS
KV_WIDTH = 2 * KEY_VALUE_HEADS * HEAD_SIZE
Q_WIDTH = QUERY_HEADS * HEAD_SIZE
EPSILON = 1e-05

PLANE = 4
LANES = 128
LINES = ("zz", "yy")
SEQ = LINES + ("cc",)

F32 = jnp.float32
BF16 = jnp.bfloat16


def dot(a, b, ca=1, cb=0, precision=None):
    return lax.dot_general(a, b, (((ca,), (cb,)), ((), ())), precision=precision, preferred_element_type=F32)


def pieces(v):
    high = v.astype(BF16).astype(F32)
    middle = (v - high).astype(BF16).astype(F32)
    return high, middle, v - high - middle


def iota(shape, dim):
    return lax.broadcasted_iota(jnp.int32, shape, dim)


def call(body, out_shape, *args, scalars=(), scratch=()):
    vmem = pl.BlockSpec(memory_space=pltpu.VMEM)
    smem = pl.BlockSpec(memory_space=pltpu.SMEM)
    return pl.pallas_call(
        body,
        out_shape=out_shape,
        in_specs=[smem] * len(scalars) + [vmem] * len(args),
        out_specs=jax.tree.map(lambda _: vmem, out_shape),
        scratch_shapes=list(scratch),
    )(*scalars, *args)


def shaped(shape, dtype):
    return jax.ShapeDtypeStruct(shape, dtype)


def selection(picks, slots):
    tokens = picks.shape[1]
    picked = jnp.broadcast_to(picks.astype(F32), (8, tokens)).astype(BF16)
    before = (iota((tokens, tokens), 0) < iota((tokens, tokens), 1)).astype(F32).astype(BF16)
    rank = dot(picked, before)[:1].astype(jnp.int32)
    hit = (iota((slots, tokens), 0) == rank) & (picks > 0)
    return hit.astype(F32).astype(BF16)


def pick_kernel(h_ref, c_ref, picks_ref, router_ref, send_ref, x_ref, cot_ref, inv_ref, gate_ref):
    lines, slots = send_ref.shape[0] // 2, send_ref.shape[1]
    width = MODEL_WIDTH // lines
    picks = picks_ref[...]
    sel = selection(picks, slots)
    x = dot(sel, h_ref[...])
    cot = dot(sel, c_ref[...])
    gate = 1.0 / (1.0 + jnp.exp(-jnp.sum(x * router_ref[...], axis=1, keepdims=True)))
    inv = lax.rsqrt(jnp.mean(x * x, axis=1, keepdims=True) + EPSILON)
    inv_ref[...] = inv
    gate_ref[...] = gate
    lane = iota((slots, LANES), 1)
    extra = jnp.where((lane == 6) & (iota((slots, 1), 0) < jnp.sum(picks)), 1.0, 0.0)
    for k, piece in enumerate(pieces(gate) + pieces(inv)):
        extra = jnp.where(lane == k, piece, extra)
    extra = extra.astype(BF16)
    x, cot = x.astype(BF16), cot.astype(BF16)
    x_ref[...] = x
    cot_ref[...] = cot
    for z in range(lines):
        cols = slice(z * width, (z + 1) * width)
        part = jnp.concatenate([x[:, cols], cot[:, cols], extra], axis=1)
        send_ref[2 * z] = part
        send_ref[2 * z + 1] = part


def put(refs, at, value):
    if len(refs) == 1:
        refs[0][at] = value
        return
    for k, ref in enumerate(refs):

        @pl.when(at == k)
        def _(ref=ref):
            ref[...] = value


def weights_kernel(at_ref, wq_ref, wkv_ref, wo_ref, *outs, lines, cpd, kpd):
    z, p = at_ref[0], at_ref[1]
    to_plane, to_lines = outs[:PLANE], outs[PLANE:]
    width = wo_ref.shape[1] // lines
    for r in range(PLANE):
        places = [PLANE * k + r for k in range(lines)]
        columns = [wq_ref[:, i * cpd : (i + 1) * cpd] for i in places]
        columns += [wkv_ref[:, i * kpd : (i + 1) * kpd] for i in places]
        put(to_plane, p ^ r, jnp.concatenate(columns, axis=1))
    for k in range(lines):
        put(to_lines, z ^ k, wo_ref[:, k * width : (k + 1) * width])


def arrange_kernel(at_ref, *refs):
    z, p = at_ref[0], at_ref[1]
    wqkv_ref, wout_ref, cols_ref = refs[-3:]
    lines, _, width = wout_ref.shape
    fb = width // PLANE
    for r in range(PLANE):
        wqkv_ref[p ^ r] = refs[r][...]
    for k in range(lines):
        rows = refs[PLANE + k][...]
        wout_ref[z ^ k] = rows
        for r in range(PLANE):
            cols_ref[p ^ r, z ^ k] = rows[:, r * fb : (r + 1) * fb]


def columns_kernel(at_ref, *refs):
    out_ref = refs[-1]
    for r in range(PLANE):
        for k in range(refs[r].shape[0]):
            out_ref[PLANE * k + (at_ref[1] ^ r)] = refs[r][k]


def load_both(core, mine_ref, other_ref, all_ref):
    for i in range(mine_ref.shape[0]):
        all_ref[2 * i + core] = mine_ref[i]
        all_ref[2 * i + 1 - core] = other_ref[i]


def heads_kernel(at_ref, mine_ref, other_ref, wqkv_ref, wout_ref, gain_ref, *refs, rows, cpd, kpd, packed):
    core = at_ref[3]
    parts = wout_ref.shape[0] if packed else 1
    part_refs, outs, got_ref = refs[:parts], refs[parts:-1], refs[-1]
    place_ref, gate_ref, normed_ref, x_ref, cot_ref = outs[:5]
    lines = wout_ref.shape[0]
    load_both(core, mine_ref, other_ref, got_ref)
    n, per, width = got_ref.shape
    slots = n * per
    half = (width - LANES) // 2
    fb = half // PLANE
    got = got_ref[...].reshape(slots, width)
    valid = got[:, 2 * half + 6 : 2 * half + 7].astype(F32) > 0.5
    ones = jnp.broadcast_to(jnp.where(valid, 1.0, 0.0), (slots, 128)).astype(BF16)
    earlier = (iota((slots, slots), 1) < iota((slots, slots), 0)).astype(F32).astype(BF16)
    rank = dot(earlier, ones)[:, :1].astype(jnp.int32)
    rank = jnp.where(valid, rank, -1)
    place = (rank == iota((slots, rows), 1)).astype(F32).astype(BF16)
    place_ref[...] = place
    compact = dot(place, got, 0, 0)
    extra = compact[:, 2 * half :]
    x, cot = compact[:, :half], compact[:, half : 2 * half]
    add_up = lambda k: extra[:, k : k + 1] + extra[:, k + 1 : k + 2] + extra[:, k + 2 : k + 3]
    gate, inv = add_up(0), add_up(3)
    normed = (x * inv * gain_ref[at_ref[0]]).astype(BF16)
    grads = (gate * cot).astype(BF16)
    three = jnp.where(iota((8, LANES), 1) < 3, 1.0, 0.0).astype(BF16)
    gate_ref[...] = dot(three, extra.astype(BF16), 1, 1)
    for r in range(PLANE):
        cols = slice(r * fb, (r + 1) * fb)

        @pl.when(at_ref[1] == r)
        def _(cols=cols):
            normed_ref[...] = normed[:, cols]
            x_ref[...] = x[:, cols].astype(BF16)
            cot_ref[...] = cot[:, cols].astype(BF16)

    wqkv = wqkv_ref[...].reshape(half, lines * (cpd + kpd))
    query = dot(normed, wqkv[:, : lines * cpd])
    kv = dot(wqkv[:, lines * cpd :], normed, 0, 1)
    grad_heads = dot(grads, wout_ref[...].reshape(lines * cpd, half), 1, 1)
    top = rows // 2
    beside = lambda m: jnp.concatenate([m[:top], m[top:]], axis=1)
    for k in range(lines):
        q_part = query[:, k * cpd : (k + 1) * cpd]
        kv_part = kv[k * kpd : (k + 1) * kpd]
        g_part = grad_heads[:, k * cpd : (k + 1) * cpd]
        if packed:
            halves = [kv_part[:, :top], kv_part[:, top:]]
            put(part_refs, at_ref[0] ^ k, jnp.concatenate([beside(q_part)] + halves + [beside(g_part)], axis=0))
        else:
            part_refs[0][k] = jnp.concatenate([q_part, g_part], axis=1)
            outs[5][k] = kv_part


def sum_kernel(*refs):
    q_ref, g_ref = refs[-2:]
    total = sum(ref[...] for ref in refs[:-2]).astype(BF16)
    lead = q_ref.shape[1]
    for i in range(q_ref.shape[0]):
        q_ref[i] = total[:lead]
        g_ref[i] = total[lead:]


def load_kv(q_all, kv_ref, kpd, top):
    n = q_all.shape[0]
    for i in range(n):
        kv_ref[i * kpd : (i + 1) * kpd, :top] = q_all[i, top : top + kpd]
        kv_ref[i * kpd : (i + 1) * kpd, top:] = q_all[i, top + kpd : top + 2 * kpd]


def probabilities(q, kt):
    heads, top, lanes = q.shape
    scale = HEAD_SIZE**-0.5

    def soft(padded, start):
        scores = dot(q.reshape(heads * top, lanes), padded).reshape(heads, top, padded.shape[1])
        allowed = iota(scores.shape, 2) <= iota(scores.shape, 1) + start
        scores = jnp.where(allowed, scores * scale, -jnp.inf)
        e = jnp.exp(scores - jnp.max(scores, axis=2, keepdims=True))
        return e / jnp.sum(e, axis=2, keepdims=True)

    zero = jnp.zeros_like(kt)
    low = soft(jnp.concatenate([kt[:, :top], zero[:, :top]], axis=0), 0)
    return low, soft(jnp.concatenate([zero, kt], axis=0), top)


def flat(x):
    return x.reshape(x.shape[0] * x.shape[1], x.shape[2])


def by_lanes(ref, first, low, high):
    top = ref.shape[0] // 2
    for start, part in ((0, low), (top, high)):
        for i in range(0, part.shape[0] // top, 2):
            both = [part[(i + j) * top : (i + j + 1) * top] for j in range(2)]
            lanes = pl.ds(pl.multiple_of((first + i) * HEAD_SIZE, 2 * HEAD_SIZE), 2 * HEAD_SIZE)
            ref[start : start + top, lanes] = jnp.concatenate(both, axis=1).astype(BF16)


def over_heads(body, heads, packed):
    if packed:
        for group in range(KEY_VALUE_HEADS):
            body(group * GROUP, GROUP, group)
    else:

        @pl.loop(0, heads // 2)
        def _(j):
            body(2 * j, 2, j // (GROUP // 2))


def forward_kernel(at_ref, *refs, packed, kpd):
    sources, (cols_ref, place_ref, cot_ref, send_ref, kv_out_ref, through_ref) = refs[:2], refs[2:8]
    probs_refs = refs[8:-2]
    q_all, mixed_ref = refs[-2:]
    heads, top = q_all.shape[0], mixed_ref.shape[0] // 2
    if packed:
        load_both(at_ref[3], *sources, q_all)
        load_kv(q_all, kv_out_ref, kpd, top)
    else:
        q_all[...] = sources[0][...]
        kv_out_ref[...] = sources[1][...]

    def some_heads(first, count, group):
        kt = kv_out_ref[pl.ds(group * HEAD_SIZE, HEAD_SIZE), :]
        vt = kv_out_ref[pl.ds((KEY_VALUE_HEADS + group) * HEAD_SIZE, HEAD_SIZE), :]
        low, high = probabilities(q_all[pl.ds(first, count), :top], kt)
        for ref, value in zip(probs_refs, (low, high)):
            ref[pl.ds(first, count)] = value
        low, high = flat(low).astype(BF16), flat(high).astype(BF16)
        by_lanes(mixed_ref, first, dot(low, vt[:, :top], 1, 1), dot(high, vt, 1, 1))

    over_heads(some_heads, heads, packed)
    n, slots, _ = send_ref.shape
    out = dot(mixed_ref[...], cols_ref[...].reshape(Q_WIDTH, cols_ref.shape[2])).astype(BF16)
    terms = cot_ref[...].astype(F32) * out.astype(F32)
    through_ref[...] = dot(jnp.ones((8, terms.shape[1]), F32), terms, 1, 1, lax.Precision.HIGHEST)
    spread = dot(place_ref[...], out).astype(BF16)
    for d in range(n):
        send_ref[d] = spread[d * slots : (d + 1) * slots]


def backward_kernel(at_ref, *refs, packed, kpd):
    count = 4 if packed else 2
    sources = refs[:count]
    kv_ref, wq_ref, wkv_ref, gain_ref, normed_ref, place_ref, out_ref = refs[count : count + 7]
    probs_refs = refs[count + 7 : -6]
    send_ref, kv_grad_ref = refs[-6:-4]
    q_all, g_all, gq_ref, gkv_ref = refs[-4:]
    heads, top = q_all.shape[0], gq_ref.shape[0] // 2
    for source, all_ref in ((sources[: count // 2], q_all), (sources[count // 2 :], g_all)):
        if packed:
            load_both(at_ref[3], *source, all_ref)
        else:
            all_ref[...] = source[0][...]
    scale = HEAD_SIZE**-0.5
    gkv_ref[...] = jnp.zeros(gkv_ref.shape, F32)

    def some_heads(first, count, group):
        some = pl.ds(first, count)
        keys = pl.ds(group * HEAD_SIZE, HEAD_SIZE)
        values = pl.ds((KEY_VALUE_HEADS + group) * HEAD_SIZE, HEAD_SIZE)
        kt, vt = kv_ref[keys, :], kv_ref[values, :]
        q, g = q_all[some, :top], flat(g_all[some])
        low, high = [ref[some] for ref in probs_refs] or probabilities(q, kt)
        q = flat(q)
        zero = jnp.zeros_like(vt)

        def back(probs, padded):
            gp = dot(g, padded).reshape(probs.shape)
            inner = jnp.sum(probs * gp, axis=2, keepdims=True)
            return flat((probs * (gp - inner)).astype(BF16))

        gs_low = back(low, jnp.concatenate([vt[:, :top], zero[:, :top]], axis=0))
        gs_high = back(high, jnp.concatenate([zero, vt], axis=0))
        low, high = flat(low).astype(BF16), flat(high).astype(BF16)
        gkv_ref[keys, :] += dot(q, gs_high, 0, 0)[HEAD_SIZE:] * scale
        gkv_ref[keys, :top] += dot(q, gs_low, 0, 0)[:HEAD_SIZE] * scale
        gkv_ref[values, :] += dot(g, high, 0, 0)[HEAD_SIZE:]
        gkv_ref[values, :top] += dot(g, low, 0, 0)[:HEAD_SIZE]
        by_lanes(gq_ref, first, dot(gs_low, kt[:, :top], 1, 1) * scale, dot(gs_high, kt, 1, 1) * scale)

    over_heads(some_heads, heads, packed)
    n, slots, fb = out_ref.shape
    gkv = gkv_ref[...].astype(BF16)
    up = (dot(gq_ref[...], wq_ref[...], 1, 1) + dot(gkv, wkv_ref[...], 0, 1)) * gain_ref[at_ref[2]]
    spread = dot(place_ref[...], up.astype(BF16)).astype(BF16)
    for d in range(n):
        send_ref[d, :, :fb] = out_ref[d]
        send_ref[d, :, fb:] = spread[d * slots : (d + 1) * slots]
    kv_grad_ref[...] = dot(normed_ref[...], gkv, 0, 1)


def router_kernel(x_ref, gate_ref, *refs):
    gate, out_ref = gate_ref[...], refs[-1]
    grad_logit = sum(ref[...] for ref in refs[:-1]) * gate * (1.0 - gate)
    out_ref[...] = dot(grad_logit, x_ref[...].astype(F32), 1, 0, lax.Precision.HIGHEST)


def place_rows(picks, rows, tokens):
    sel = selection(picks, rows.shape[0])
    taken = dot(sel, jnp.ones((rows.shape[0], 128), BF16), 0, 0)[:, :1] > 0.5
    return jnp.where(taken, dot(sel, rows, 0, 0), tokens.astype(F32)).astype(BF16)


def add_kernel(a_ref, b_ref, out_ref):
    out_ref[...] = a_ref[...] + b_ref[...]


def finish_kernel(
    h_ref, c_ref, picks_ref, router_ref, gate_ref, x_ref, cot_ref, inv_ref, got_ref, part_ref, other_ref,
    mixed_ref, grad_ref, router_grad_ref
):
    router_grad_ref[...] = part_ref[:1] + other_ref[:1]
    n, _, width = got_ref.shape
    fb = width // 2
    take = lambda k: jnp.concatenate([got_ref[d, :, k * fb : (k + 1) * fb] for d in range(n)], axis=1).astype(F32)
    out, up = take(0), take(1)
    x, inv, gate = x_ref[...].astype(F32), inv_ref[...], gate_ref[...]
    picks = picks_ref[...]
    mixed_ref[...] = place_rows(picks, (x + gate * out).astype(BF16), h_ref[...])
    cot = cot_ref[...].astype(F32)
    grad_logit = jnp.sum(cot * out, axis=1, keepdims=True) * gate * (1.0 - gate)
    grad_block = inv * up - x * inv**3 * jnp.mean(up * x, axis=1, keepdims=True)
    grad_block = grad_block.astype(BF16).astype(F32)
    rows = (cot + grad_logit * router_ref[...] + grad_block).astype(BF16)
    grad_ref[...] = place_rows(picks, rows, c_ref[...])


def exchange(x, axes):
    return lax.all_to_all(x, axes, 0, 0, tiled=True)


def swap(x, n, bit):
    return lax.ppermute(x, SEQ, [(i, i ^ bit) for i in range(n)])


def block(hidden, cotangent, picks, gain, router, w_query, w_kv, w_out):
    lines = lax.axis_size("zz")
    n = lines * PLANE
    dp = lax.axis_size("dp")
    z, core = lax.axis_index("zz"), lax.axis_index("cc")
    p = 2 * lax.axis_index("yy") + core
    me = PLANE * z + p
    where = jnp.stack([z, p, me, core]).astype(jnp.int32)
    hidden, cotangent = hidden[0], cotangent[0]
    tokens = hidden.shape[0]
    slots = tokens // 4
    rows = n * (tokens // 8)
    top = rows // 2
    fb = MODEL_WIDTH // n
    cpd = Q_WIDTH // n
    kpd = KV_WIDTH // n
    packed = cpd == HEAD_SIZE
    as_row = lambda v: v.reshape(1, -1)

    lines_apart = lines <= 4
    to_plane = [shaped((fb, lines * (cpd + kpd)), BF16)] * PLANE
    to_lines = [shaped((cpd, PLANE * fb), BF16)] * lines if lines_apart else [shaped((lines, cpd, PLANE * fb), BF16)]
    out = call(
        functools.partial(weights_kernel, lines=lines, cpd=cpd, kpd=kpd),
        tuple(to_plane + to_lines),
        w_query,
        w_kv,
        w_out,
        scalars=(where,),
    )
    to_plane, to_lines = out[:PLANE], out[PLANE:]
    if not lines_apart:
        to_lines = [to_lines[0][k] for k in range(lines)]
    wqkv = [to_plane[0]] + [swap(to_plane[r], n, r) for r in range(1, PLANE)]
    wout = [to_lines[0]] + [swap(to_lines[k], n, PLANE * k) for k in range(1, lines)]
    wqkv, wout, cols = call(
        arrange_kernel,
        (
            shaped((PLANE, fb, lines * (cpd + kpd)), BF16),
            shaped((lines, cpd, PLANE * fb), BF16),
            shaped((PLANE, lines, cpd, fb), BF16),
        ),
        *wqkv,
        *wout,
        scalars=(where,),
    )

    send, x, cot, inv, gate = call(
        pick_kernel,
        (
            shaped((2 * lines, slots, 2 * PLANE * fb + LANES), BF16),
            shaped((slots, MODEL_WIDTH), BF16),
            shaped((slots, MODEL_WIDTH), BF16),
            shaped((slots, 1), F32),
            shaped((slots, 1), F32),
        ),
        hidden,
        cotangent,
        picks,
        as_row(router),
    )
    mine = exchange(send, LINES)
    other = swap(mine, n, 1)

    parts = [(top + 2 * kpd + top, 2 * cpd)] * lines if packed else [(lines, rows, 2 * cpd)]
    outs = [shaped(part, F32) for part in parts] + [
        shaped((n * slots, rows), BF16),
        shaped((8, rows), F32),
    ]
    outs += [shaped((rows, fb), BF16)] * 3
    if not packed:
        outs += [shaped((lines, kpd, rows), F32)]
    out = call(
        functools.partial(heads_kernel, rows=rows, cpd=cpd, kpd=kpd, packed=packed),
        tuple(outs),
        mine,
        other,
        wqkv,
        wout,
        gain.reshape(lines, 1, PLANE * fb),
        scalars=(where,),
        scratch=(pltpu.VMEM((n, slots, 2 * PLANE * fb + LANES), BF16),),
    )
    parts, (place, gate_rows, normed, own_x, own_cot, *kv_part) = out[: len(parts)], out[len(parts) :]
    cols = [cols[0]] + [swap(cols[r], n, r) for r in range(1, PLANE)]
    cols = call(columns_kernel, shaped((n, cpd, fb), BF16), *cols, scalars=(where,))
    if packed:
        parts = [parts[0]] + [swap(parts[k], n, PLANE * k) for k in range(1, lines)]
        lead = top + 2 * kpd
        q_pack, g_pack = call(
            sum_kernel, (shaped((2 * lines, lead, 2 * cpd), BF16), shaped((2 * lines, top, 2 * cpd), BF16)), *parts
        )
        q_refs = exchange(q_pack, LINES)
        q_refs = (q_refs, swap(q_refs, n, 1))
        g_refs = exchange(g_pack, LINES)
        g_refs = (g_refs, swap(g_refs, n, 1))
        kv_refs = ()
    else:
        per = HEAD_SIZE // cpd
        everything = jnp.sum(exchange(parts[0], "zz"), axis=0).astype(BF16)
        everything = lax.all_gather(everything, SEQ, axis=0).reshape(QUERY_HEADS, per, 2, top, 2, cpd)
        everything = everything.transpose(4, 0, 3, 2, 1, 5).reshape(2, QUERY_HEADS, top, 2 * HEAD_SIZE)
        q_refs, g_refs = (everything[0],), (everything[1],)
        kv_part = lax.all_to_all(kv_part[0], "zz", 0, 0, tiled=True)
        kv_part = jnp.sum(kv_part, axis=0).astype(BF16)
        kv_refs = (lax.all_gather(kv_part, SEQ, axis=0, tiled=True),)
    q_scratch = pltpu.VMEM((QUERY_HEADS, top + (2 * kpd if packed else 0), 2 * HEAD_SIZE), BF16)

    probs = (shaped((QUERY_HEADS, top, top), F32), shaped((QUERY_HEADS, top, rows), F32)) if packed else ()
    out, kv_all, through, *probs = call(
        functools.partial(forward_kernel, packed=packed, kpd=kpd),
        (
            shaped((n, slots, fb), BF16),
            shaped((KV_WIDTH, rows), BF16),
            shaped((8, rows), F32),
            *probs,
        ),
        *q_refs,
        *kv_refs,
        cols,
        place,
        own_cot,
        scalars=(where,),
        scratch=(q_scratch, pltpu.VMEM((rows, Q_WIDTH), BF16)),
    )
    through = [through] + [swap(through, n, r) for r in range(1, PLANE)]
    send, kv_part = call(
        functools.partial(backward_kernel, packed=packed, kpd=kpd),
        (shaped((n, slots, 2 * fb), BF16), shaped((fb, KV_WIDTH), F32)),
        *q_refs,
        *g_refs,
        kv_all,
        w_query,
        w_kv,
        gain.reshape(n, 1, fb),
        normed,
        place,
        out,
        *probs,
        scalars=(where,),
        scratch=(
            q_scratch,
            pltpu.VMEM((QUERY_HEADS, top, 2 * HEAD_SIZE), BF16),
            pltpu.VMEM((rows, Q_WIDTH), BF16),
            pltpu.VMEM((KV_WIDTH, rows), F32),
        ),
    )
    got = exchange(send, SEQ)
    through = sum(through[1:], through[0])
    through = [through] + [swap(through, n, PLANE * k) for k in range(1, lines)]
    router_part = call(router_kernel, shaped((8, fb), F32), own_x, gate_rows, *through)
    if dp == 2:
        pair = [(0, 1), (1, 0)]
        other = lax.ppermute(kv_part, "dp", pair)
        kv_grad = call(add_kernel, shaped((fb, KV_WIDTH), F32), kv_part, other)
        router_other = lax.ppermute(router_part, "dp", pair)
    else:
        kv_grad, router_part = lax.psum(kv_part, "dp"), lax.psum(router_part, "dp")
        router_other = jnp.zeros_like(router_part)
    mixed, input_grad, router_grad = call(
        finish_kernel,
        (
            shaped((tokens, MODEL_WIDTH), BF16),
            shaped((tokens, MODEL_WIDTH), BF16),
            shaped((1, fb), F32),
        ),
        hidden,
        cotangent,
        picks,
        as_row(router),
        gate,
        x,
        cot,
        inv,
        got,
        router_part,
        router_other,
    )
    return mixed[None], input_grad[None], kv_grad, router_grad.reshape(fb)


def solution(mesh):
    dp, n = mesh.shape["dp"], mesh.shape["seq"]
    split = Mesh(mesh.devices.reshape(dp, n // PLANE, PLANE // 2, 2), ("dp",) + SEQ)
    rows = P("dp", SEQ, None)
    return jax.shard_map(
        block,
        mesh=split,
        in_specs=(rows, rows, P("dp", SEQ), P(), P(), P(SEQ, None), P(SEQ, None), P(SEQ, None)),
        out_specs=(rows, rows, P(SEQ, None), P(SEQ)),
        check_vma=False,
    )
```

```python
import functools

import jax
import jax.numpy as jnp
from jax import lax
from jax.experimental import pallas as pl
from jax.experimental.pallas import tpu as pltpu
from jax.sharding import Mesh, PartitionSpec as P


MODEL_WIDTH = 2048
QUERY_HEADS = 16
KEY_VALUE_HEADS = 2
HEAD_SIZE = 64
GROUP = QUERY_HEADS // KEY_VALUE_HEADS
KV_WIDTH = 2 * KEY_VALUE_HEADS * HEAD_SIZE
Q_WIDTH = QUERY_HEADS * HEAD_SIZE
EPSILON = 1e-05

PLANE = 4
LANES = 128
LINES = ("zz", "yy")
SEQ = LINES + ("cc",)

F32 = jnp.float32
BF16 = jnp.bfloat16


def dot(a, b, ca=1, cb=0, precision=None):
    return lax.dot_general(a, b, (((ca,), (cb,)), ((), ())), precision=precision, preferred_element_type=F32)


def pieces(v):
    high = v.astype(BF16).astype(F32)
    middle = (v - high).astype(BF16).astype(F32)
    return high, middle, v - high - middle


def iota(shape, dim):
    return lax.broadcasted_iota(jnp.int32, shape, dim)


def call(body, out_shape, *args, scalars=(), scratch=()):
    vmem = pl.BlockSpec(memory_space=pltpu.VMEM)
    smem = pl.BlockSpec(memory_space=pltpu.SMEM)
    return pl.pallas_call(
        body,
        out_shape=out_shape,
        in_specs=[smem] * len(scalars) + [vmem] * len(args),
        out_specs=jax.tree.map(lambda _: vmem, out_shape),
        scratch_shapes=list(scratch),
    )(*scalars, *args)


def shaped(shape, dtype):
    return jax.ShapeDtypeStruct(shape, dtype)


def selection(picks, slots):
    tokens = picks.shape[1]
    picked = jnp.broadcast_to(picks.astype(F32), (8, tokens)).astype(BF16)
    before = (iota((tokens, tokens), 0) < iota((tokens, tokens), 1)).astype(F32).astype(BF16)
    rank = dot(picked, before)[:1].astype(jnp.int32)
    hit = (iota((slots, tokens), 0) == rank) & (picks > 0)
    return hit.astype(F32).astype(BF16)


def pick_kernel(h_ref, c_ref, picks_ref, router_ref, send_ref, x_ref, cot_ref, inv_ref, gate_ref):
    lines, slots = send_ref.shape[0] // 2, send_ref.shape[1]
    width = MODEL_WIDTH // lines
    picks = picks_ref[...]
    sel = selection(picks, slots)
    x = dot(sel, h_ref[...])
    cot = dot(sel, c_ref[...])
    gate = 1.0 / (1.0 + jnp.exp(-jnp.sum(x * router_ref[...], axis=1, keepdims=True)))
    inv = lax.rsqrt(jnp.mean(x * x, axis=1, keepdims=True) + EPSILON)
    inv_ref[...] = inv
    gate_ref[...] = gate
    lane = iota((slots, LANES), 1)
    extra = jnp.where((lane == 6) & (iota((slots, 1), 0) < jnp.sum(picks)), 1.0, 0.0)
    for k, piece in enumerate(pieces(gate) + pieces(inv)):
        extra = jnp.where(lane == k, piece, extra)
    extra = extra.astype(BF16)
    x, cot = x.astype(BF16), cot.astype(BF16)
    x_ref[...] = x
    cot_ref[...] = cot
    for z in range(lines):
        cols = slice(z * width, (z + 1) * width)
        part = jnp.concatenate([x[:, cols], cot[:, cols], extra], axis=1)
        send_ref[2 * z] = part
        send_ref[2 * z + 1] = part


def put(refs, at, value):
    if len(refs) == 1:
        refs[0][at] = value
        return
    for k, ref in enumerate(refs):

        @pl.when(at == k)
        def _(ref=ref):
            ref[...] = value


def weights_kernel(at_ref, wq_ref, wkv_ref, wo_ref, *outs, lines, cpd, kpd):
    z, p = at_ref[0], at_ref[1]
    to_plane, to_lines = outs[:PLANE], outs[PLANE:]
    width = wo_ref.shape[1] // lines
    for r in range(PLANE):
        places = [PLANE * k + r for k in range(lines)]
        columns = [wq_ref[:, i * cpd : (i + 1) * cpd] for i in places]
        columns += [wkv_ref[:, i * kpd : (i + 1) * kpd] for i in places]
        put(to_plane, p ^ r, jnp.concatenate(columns, axis=1))
    for k in range(lines):
        put(to_lines, z ^ k, wo_ref[:, k * width : (k + 1) * width])


def arrange_kernel(at_ref, *refs):
    for r in range(PLANE):
        refs[-1][at_ref[1] ^ r] = refs[r][...]


def arrange_out_kernel(at_ref, *refs):
    z, p = at_ref[0], at_ref[1]
    wout_ref, cols_ref = refs[-2:]
    lines, _, width = wout_ref.shape
    fb = width // PLANE
    for k in range(lines):
        rows = refs[k][...]
        wout_ref[z ^ k] = rows
        for r in range(PLANE):
            cols_ref[p ^ r, z ^ k] = rows[:, r * fb : (r + 1) * fb]


def columns_kernel(at_ref, *refs):
    out_ref = refs[-1]
    for r in range(PLANE):
        for k in range(refs[r].shape[0]):
            out_ref[PLANE * k + (at_ref[1] ^ r)] = refs[r][k]


def load_both(core, mine_ref, other_ref, all_ref):
    for i in range(mine_ref.shape[0]):
        all_ref[2 * i + core] = mine_ref[i]
        all_ref[2 * i + 1 - core] = other_ref[i]


def heads_kernel(at_ref, mine_ref, other_ref, wqkv_ref, wout_ref, gain_ref, *refs, rows, cpd, kpd, packed):
    core = at_ref[3]
    parts = wout_ref.shape[0] if packed else 1
    part_refs, outs, got_ref = refs[:parts], refs[parts:-1], refs[-1]
    place_ref, gate_ref, normed_ref, x_ref, cot_ref = outs[:5]
    lines = wout_ref.shape[0]
    load_both(core, mine_ref, other_ref, got_ref)
    n, per, width = got_ref.shape
    slots = n * per
    half = (width - LANES) // 2
    fb = half // PLANE
    got = got_ref[...].reshape(slots, width)
    valid = got[:, 2 * half + 6 : 2 * half + 7].astype(F32) > 0.5
    ones = jnp.broadcast_to(jnp.where(valid, 1.0, 0.0), (slots, 128)).astype(BF16)
    earlier = (iota((slots, slots), 1) < iota((slots, slots), 0)).astype(F32).astype(BF16)
    rank = dot(earlier, ones)[:, :1].astype(jnp.int32)
    rank = jnp.where(valid, rank, -1)
    place = (rank == iota((slots, rows), 1)).astype(F32).astype(BF16)
    place_ref[...] = place
    compact = dot(place, got, 0, 0)
    extra = compact[:, 2 * half :]
    x, cot = compact[:, :half], compact[:, half : 2 * half]
    add_up = lambda k: extra[:, k : k + 1] + extra[:, k + 1 : k + 2] + extra[:, k + 2 : k + 3]
    gate, inv = add_up(0), add_up(3)
    normed = (x * inv * gain_ref[at_ref[0]]).astype(BF16)
    grads = (gate * cot).astype(BF16)
    three = jnp.where(iota((8, LANES), 1) < 3, 1.0, 0.0).astype(BF16)
    gate_ref[...] = dot(three, extra.astype(BF16), 1, 1)
    for r in range(PLANE):
        cols = slice(r * fb, (r + 1) * fb)

        @pl.when(at_ref[1] == r)
        def _(cols=cols):
            normed_ref[...] = normed[:, cols]
            x_ref[...] = x[:, cols].astype(BF16)
            cot_ref[...] = cot[:, cols].astype(BF16)

    wqkv = wqkv_ref[...].reshape(half, lines * (cpd + kpd))
    query = dot(normed, wqkv[:, : lines * cpd])
    kv = dot(wqkv[:, lines * cpd :], normed, 0, 1)
    grad_heads = dot(grads, wout_ref[...].reshape(lines * cpd, half), 1, 1)
    top = rows // 2
    beside = lambda m: jnp.concatenate([m[:top], m[top:]], axis=1)
    for k in range(lines):
        q_part = query[:, k * cpd : (k + 1) * cpd]
        kv_part = kv[k * kpd : (k + 1) * kpd]
        g_part = grad_heads[:, k * cpd : (k + 1) * cpd]
        if packed:
            halves = [kv_part[:, :top], kv_part[:, top:]]
            put(part_refs, at_ref[0] ^ k, jnp.concatenate([beside(q_part)] + halves + [beside(g_part)], axis=0))
        else:
            part_refs[0][k] = jnp.concatenate([q_part, g_part], axis=1)
            outs[5][k] = kv_part


def sum_kernel(*refs):
    q_ref, g_ref = refs[-2:]
    total = sum(ref[...] for ref in refs[:-2]).astype(BF16)
    lead = q_ref.shape[1]
    for i in range(q_ref.shape[0]):
        q_ref[i] = total[:lead]
        g_ref[i] = total[lead:]


def load_kv(q_all, kv_ref, kpd, top):
    n = q_all.shape[0]
    for i in range(n):
        kv_ref[i * kpd : (i + 1) * kpd, :top] = q_all[i, top : top + kpd]
        kv_ref[i * kpd : (i + 1) * kpd, top:] = q_all[i, top + kpd : top + 2 * kpd]


def probabilities(q, kt):
    heads, top, lanes = q.shape
    scale = HEAD_SIZE**-0.5

    def soft(padded, start):
        scores = dot(q.reshape(heads * top, lanes), padded).reshape(heads, top, padded.shape[1])
        allowed = iota(scores.shape, 2) <= iota(scores.shape, 1) + start
        scores = jnp.where(allowed, scores * scale, -jnp.inf)
        e = jnp.exp(scores - jnp.max(scores, axis=2, keepdims=True))
        return e / jnp.sum(e, axis=2, keepdims=True)

    zero = jnp.zeros_like(kt)
    low = soft(jnp.concatenate([kt[:, :top], zero[:, :top]], axis=0), 0)
    return low, soft(jnp.concatenate([zero, kt], axis=0), top)


def flat(x):
    return x.reshape(x.shape[0] * x.shape[1], x.shape[2])


def by_lanes(ref, first, low, high):
    top = ref.shape[0] // 2
    for start, part in ((0, low), (top, high)):
        for i in range(0, part.shape[0] // top, 2):
            both = [part[(i + j) * top : (i + j + 1) * top] for j in range(2)]
            lanes = pl.ds(pl.multiple_of((first + i) * HEAD_SIZE, 2 * HEAD_SIZE), 2 * HEAD_SIZE)
            ref[start : start + top, lanes] = jnp.concatenate(both, axis=1).astype(BF16)


def over_heads(body, heads, packed):
    if packed:
        for group in range(KEY_VALUE_HEADS):
            body(group * GROUP, GROUP, group)
    else:

        @pl.loop(0, heads // 2)
        def _(j):
            body(2 * j, 2, j // (GROUP // 2))


def forward_kernel(at_ref, *refs, packed, kpd):
    sources, (cols_ref, place_ref, cot_ref, send_ref, kv_out_ref, through_ref) = refs[:2], refs[2:8]
    probs_refs = refs[8:-2]
    q_all, mixed_ref = refs[-2:]
    heads, top = q_all.shape[0], mixed_ref.shape[0] // 2
    if packed:
        load_both(at_ref[3], *sources, q_all)
        load_kv(q_all, kv_out_ref, kpd, top)
    else:
        q_all[...] = sources[0][...]
        kv_out_ref[...] = sources[1][...]

    def some_heads(first, count, group):
        kt = kv_out_ref[pl.ds(group * HEAD_SIZE, HEAD_SIZE), :]
        vt = kv_out_ref[pl.ds((KEY_VALUE_HEADS + group) * HEAD_SIZE, HEAD_SIZE), :]
        low, high = probabilities(q_all[pl.ds(first, count), :top], kt)
        for ref, value in zip(probs_refs, (low, high)):
            ref[pl.ds(first, count)] = value
        low, high = flat(low).astype(BF16), flat(high).astype(BF16)
        by_lanes(mixed_ref, first, dot(low, vt[:, :top], 1, 1), dot(high, vt, 1, 1))

    over_heads(some_heads, heads, packed)
    n, slots, _ = send_ref.shape
    out = dot(mixed_ref[...], cols_ref[...].reshape(Q_WIDTH, cols_ref.shape[2])).astype(BF16)
    terms = cot_ref[...].astype(F32) * out.astype(F32)
    through_ref[...] = dot(jnp.ones((8, terms.shape[1]), F32), terms, 1, 1, lax.Precision.HIGHEST)
    spread = dot(place_ref[...], out).astype(BF16)
    for d in range(n):
        send_ref[d] = spread[d * slots : (d + 1) * slots]


def backward_kernel(at_ref, *refs, packed, kpd):
    count = 4 if packed else 2
    sources = refs[:count]
    kv_ref, wq_ref, wkv_ref, gain_ref, normed_ref, place_ref, out_ref = refs[count : count + 7]
    probs_refs = refs[count + 7 : -6]
    send_ref, kv_grad_ref = refs[-6:-4]
    q_all, g_all, gq_ref, gkv_ref = refs[-4:]
    heads, top = q_all.shape[0], gq_ref.shape[0] // 2
    for source, all_ref in ((sources[: count // 2], q_all), (sources[count // 2 :], g_all)):
        if packed:
            load_both(at_ref[3], *source, all_ref)
        else:
            all_ref[...] = source[0][...]
    scale = HEAD_SIZE**-0.5
    gkv_ref[...] = jnp.zeros(gkv_ref.shape, F32)

    def some_heads(first, count, group):
        some = pl.ds(first, count)
        keys = pl.ds(group * HEAD_SIZE, HEAD_SIZE)
        values = pl.ds((KEY_VALUE_HEADS + group) * HEAD_SIZE, HEAD_SIZE)
        kt, vt = kv_ref[keys, :], kv_ref[values, :]
        q, g = q_all[some, :top], flat(g_all[some])
        low, high = [ref[some] for ref in probs_refs] or probabilities(q, kt)
        q = flat(q)
        zero = jnp.zeros_like(vt)

        def back(probs, padded):
            gp = dot(g, padded).reshape(probs.shape)
            inner = jnp.sum(probs * gp, axis=2, keepdims=True)
            return flat((probs * (gp - inner)).astype(BF16))

        gs_low = back(low, jnp.concatenate([vt[:, :top], zero[:, :top]], axis=0))
        gs_high = back(high, jnp.concatenate([zero, vt], axis=0))
        low, high = flat(low).astype(BF16), flat(high).astype(BF16)
        gkv_ref[keys, :] += dot(q, gs_high, 0, 0)[HEAD_SIZE:] * scale
        gkv_ref[keys, :top] += dot(q, gs_low, 0, 0)[:HEAD_SIZE] * scale
        gkv_ref[values, :] += dot(g, high, 0, 0)[HEAD_SIZE:]
        gkv_ref[values, :top] += dot(g, low, 0, 0)[:HEAD_SIZE]
        by_lanes(gq_ref, first, dot(gs_low, kt[:, :top], 1, 1) * scale, dot(gs_high, kt, 1, 1) * scale)

    over_heads(some_heads, heads, packed)
    n, slots, fb = out_ref.shape
    gkv = gkv_ref[...].astype(BF16)
    up = (dot(gq_ref[...], wq_ref[...], 1, 1) + dot(gkv, wkv_ref[...], 0, 1)) * gain_ref[at_ref[2]]
    spread = dot(place_ref[...], up.astype(BF16)).astype(BF16)
    for d in range(n):
        send_ref[d, :, :fb] = out_ref[d]
        send_ref[d, :, fb:] = spread[d * slots : (d + 1) * slots]
    kv_grad_ref[...] = dot(normed_ref[...], gkv, 0, 1)


def router_kernel(x_ref, gate_ref, *refs):
    gate, out_ref = gate_ref[...], refs[-1]
    grad_logit = sum(ref[...] for ref in refs[:-1]) * gate * (1.0 - gate)
    out_ref[...] = dot(grad_logit, x_ref[...].astype(F32), 1, 0, lax.Precision.HIGHEST)


def place_rows(picks, rows, tokens):
    sel = selection(picks, rows.shape[0])
    taken = dot(sel, jnp.ones((rows.shape[0], 128), BF16), 0, 0)[:, :1] > 0.5
    return jnp.where(taken, dot(sel, rows, 0, 0), tokens.astype(F32)).astype(BF16)


def add_kernel(a_ref, b_ref, out_ref):
    out_ref[...] = a_ref[...] + b_ref[...]


def finish_kernel(
    h_ref, c_ref, picks_ref, router_ref, gate_ref, x_ref, cot_ref, inv_ref, got_ref, part_ref, other_ref,
    mixed_ref, grad_ref, router_grad_ref
):
    router_grad_ref[...] = part_ref[:1] + other_ref[:1]
    n, _, width = got_ref.shape
    fb = width // 2
    take = lambda k: jnp.concatenate([got_ref[d, :, k * fb : (k + 1) * fb] for d in range(n)], axis=1).astype(F32)
    out, up = take(0), take(1)
    x, inv, gate = x_ref[...].astype(F32), inv_ref[...], gate_ref[...]
    picks = picks_ref[...]
    mixed_ref[...] = place_rows(picks, (x + gate * out).astype(BF16), h_ref[...])
    cot = cot_ref[...].astype(F32)
    grad_logit = jnp.sum(cot * out, axis=1, keepdims=True) * gate * (1.0 - gate)
    grad_block = inv * up - x * inv**3 * jnp.mean(up * x, axis=1, keepdims=True)
    grad_block = grad_block.astype(BF16).astype(F32)
    rows = (cot + grad_logit * router_ref[...] + grad_block).astype(BF16)
    grad_ref[...] = place_rows(picks, rows, c_ref[...])


def exchange(x, axes):
    return lax.all_to_all(x, axes, 0, 0, tiled=True)


def swap(x, n, bit):
    return lax.ppermute(x, SEQ, [(i, i ^ bit) for i in range(n)])


def block(hidden, cotangent, picks, gain, router, w_query, w_kv, w_out):
    lines = lax.axis_size("zz")
    n = lines * PLANE
    dp = lax.axis_size("dp")
    z, core = lax.axis_index("zz"), lax.axis_index("cc")
    p = 2 * lax.axis_index("yy") + core
    me = PLANE * z + p
    where = jnp.stack([z, p, me, core]).astype(jnp.int32)
    hidden, cotangent = hidden[0], cotangent[0]
    tokens = hidden.shape[0]
    slots = tokens // 4
    rows = n * (tokens // 8)
    top = rows // 2
    fb = MODEL_WIDTH // n
    cpd = Q_WIDTH // n
    kpd = KV_WIDTH // n
    packed = cpd == HEAD_SIZE
    as_row = lambda v: v.reshape(1, -1)

    lines_apart = lines <= 4
    to_plane = [shaped((fb, lines * (cpd + kpd)), BF16)] * PLANE
    to_lines = [shaped((cpd, PLANE * fb), BF16)] * lines if lines_apart else [shaped((lines, cpd, PLANE * fb), BF16)]
    out = call(
        functools.partial(weights_kernel, lines=lines, cpd=cpd, kpd=kpd),
        tuple(to_plane + to_lines),
        w_query,
        w_kv,
        w_out,
        scalars=(where,),
    )
    to_plane, to_lines = out[:PLANE], out[PLANE:]
    if not lines_apart:
        to_lines = [to_lines[0][k] for k in range(lines)]
    wqkv = [to_plane[0]] + [swap(to_plane[r], n, r) for r in range(1, PLANE)]
    wout = [to_lines[0]] + [swap(to_lines[k], n, PLANE * k) for k in range(1, lines)]
    wqkv = call(arrange_kernel, shaped((PLANE, fb, lines * (cpd + kpd)), BF16), *wqkv, scalars=(where,))
    wout, cols = call(
        arrange_out_kernel,
        (shaped((lines, cpd, PLANE * fb), BF16), shaped((PLANE, lines, cpd, fb), BF16)),
        *wout,
        scalars=(where,),
    )

    send, x, cot, inv, gate = call(
        pick_kernel,
        (
            shaped((2 * lines, slots, 2 * PLANE * fb + LANES), BF16),
            shaped((slots, MODEL_WIDTH), BF16),
            shaped((slots, MODEL_WIDTH), BF16),
            shaped((slots, 1), F32),
            shaped((slots, 1), F32),
        ),
        hidden,
        cotangent,
        picks,
        as_row(router),
    )
    mine = exchange(send, LINES)
    other = swap(mine, n, 1)

    parts = [(top + 2 * kpd + top, 2 * cpd)] * lines if packed else [(lines, rows, 2 * cpd)]
    outs = [shaped(part, F32) for part in parts] + [
        shaped((n * slots, rows), BF16),
        shaped((8, rows), F32),
    ]
    outs += [shaped((rows, fb), BF16)] * 3
    if not packed:
        outs += [shaped((lines, kpd, rows), F32)]
    out = call(
        functools.partial(heads_kernel, rows=rows, cpd=cpd, kpd=kpd, packed=packed),
        tuple(outs),
        mine,
        other,
        wqkv,
        wout,
        gain.reshape(lines, 1, PLANE * fb),
        scalars=(where,),
        scratch=(pltpu.VMEM((n, slots, 2 * PLANE * fb + LANES), BF16),),
    )
    parts, (place, gate_rows, normed, own_x, own_cot, *kv_part) = out[: len(parts)], out[len(parts) :]
    cols = [cols[0]] + [swap(cols[r], n, r) for r in range(1, PLANE)]
    cols = call(columns_kernel, shaped((n, cpd, fb), BF16), *cols, scalars=(where,))
    if packed:
        parts = [parts[0]] + [swap(parts[k], n, PLANE * k) for k in range(1, lines)]
        lead = top + 2 * kpd
        q_pack, g_pack = call(
            sum_kernel, (shaped((2 * lines, lead, 2 * cpd), BF16), shaped((2 * lines, top, 2 * cpd), BF16)), *parts
        )
        q_refs = exchange(q_pack, LINES)
        q_refs = (q_refs, swap(q_refs, n, 1))
        g_refs = exchange(g_pack, LINES)
        g_refs = (g_refs, swap(g_refs, n, 1))
        kv_refs = ()
    else:
        per = HEAD_SIZE // cpd
        everything = jnp.sum(exchange(parts[0], "zz"), axis=0).astype(BF16)
        everything = lax.all_gather(everything, SEQ, axis=0).reshape(QUERY_HEADS, per, 2, top, 2, cpd)
        everything = everything.transpose(4, 0, 3, 2, 1, 5).reshape(2, QUERY_HEADS, top, 2 * HEAD_SIZE)
        q_refs, g_refs = (everything[0],), (everything[1],)
        kv_part = lax.all_to_all(kv_part[0], "zz", 0, 0, tiled=True)
        kv_part = jnp.sum(kv_part, axis=0).astype(BF16)
        kv_refs = (lax.all_gather(kv_part, SEQ, axis=0, tiled=True),)
    q_scratch = pltpu.VMEM((QUERY_HEADS, top + (2 * kpd if packed else 0), 2 * HEAD_SIZE), BF16)

    probs = (shaped((QUERY_HEADS, top, top), F32), shaped((QUERY_HEADS, top, rows), F32)) if packed else ()
    out, kv_all, through, *probs = call(
        functools.partial(forward_kernel, packed=packed, kpd=kpd),
        (
            shaped((n, slots, fb), BF16),
            shaped((KV_WIDTH, rows), BF16),
            shaped((8, rows), F32),
            *probs,
        ),
        *q_refs,
        *kv_refs,
        cols,
        place,
        own_cot,
        scalars=(where,),
        scratch=(q_scratch, pltpu.VMEM((rows, Q_WIDTH), BF16)),
    )
    through = [through] + [swap(through, n, r) for r in range(1, PLANE)]
    send, kv_part = call(
        functools.partial(backward_kernel, packed=packed, kpd=kpd),
        (shaped((n, slots, 2 * fb), BF16), shaped((fb, KV_WIDTH), F32)),
        *q_refs,
        *g_refs,
        kv_all,
        w_query,
        w_kv,
        gain.reshape(n, 1, fb),
        normed,
        place,
        out,
        *probs,
        scalars=(where,),
        scratch=(
            q_scratch,
            pltpu.VMEM((QUERY_HEADS, top, 2 * HEAD_SIZE), BF16),
            pltpu.VMEM((rows, Q_WIDTH), BF16),
            pltpu.VMEM((KV_WIDTH, rows), F32),
        ),
    )
    got = exchange(send, SEQ)
    through = sum(through[1:], through[0])
    through = [through] + [swap(through, n, PLANE * k) for k in range(1, lines)]
    router_part = call(router_kernel, shaped((8, fb), F32), own_x, gate_rows, *through)
    if dp == 2:
        pair = [(0, 1), (1, 0)]
        other = lax.ppermute(kv_part, "dp", pair)
        kv_grad = call(add_kernel, shaped((fb, KV_WIDTH), F32), kv_part, other)
        router_other = lax.ppermute(router_part, "dp", pair)
    else:
        kv_grad, router_part = lax.psum(kv_part, "dp"), lax.psum(router_part, "dp")
        router_other = jnp.zeros_like(router_part)
    mixed, input_grad, router_grad = call(
        finish_kernel,
        (
            shaped((tokens, MODEL_WIDTH), BF16),
            shaped((tokens, MODEL_WIDTH), BF16),
            shaped((1, fb), F32),
        ),
        hidden,
        cotangent,
        picks,
        as_row(router),
        gate,
        x,
        cot,
        inv,
        got,
        router_part,
        router_other,
    )
    return mixed[None], input_grad[None], kv_grad, router_grad.reshape(fb)


def solution(mesh):
    dp, n = mesh.shape["dp"], mesh.shape["seq"]
    split = Mesh(mesh.devices.reshape(dp, n // PLANE, PLANE // 2, 2), ("dp",) + SEQ)
    rows = P("dp", SEQ, None)
    return jax.shard_map(
        block,
        mesh=split,
        in_specs=(rows, rows, P("dp", SEQ), P(), P(), P(SEQ, None), P(SEQ, None), P(SEQ, None)),
        out_specs=(rows, rows, P(SEQ, None), P(SEQ)),
        check_vma=False,
    )
```
